32 devices in a mesh: mode: 8 (over z, x), row: 4 (over y, core).
Axes of the slice: x: 2, y: 2, z: 4, core: 2. Of those that a mesh axis runs over, the one named last changes fastest.
Arguments:
- forward: bfloat16 [64, 8, 2, 512], P('mode', 'row'), may hold values from -6 to 6
- backward: bfloat16 [64, 8, 2, 512], P('mode', 'row'), may hold values from -6 to 6
- propagator: bfloat16 [2, 512, 512], replicated, may hold values from -0.1875 to 0.1875
- row_taps: float32 [2, 3], replicated, may hold values from -3 to 3
- phase_masks: float32 [7, 8, 512], P(None, 'row'), may hold values from -3.140625 to 3.140625
- plane_index: int32 [4], replicated, may hold values from 0 to 6
- wave_ratio: float32 [4], replicated, may hold values from 0.7 to 1.4
- pair_list: int32 [80, 2], replicated, may hold values from 0 to 15, as said below
Outputs:
- coupling: float32 [2, 64, 64], P(None, 'mode')
- mask_grad: float32 [4, 8, 512], P(None, 'row')
The draws below stay inside these ranges and needn't reach their ends.
Inputs may be any that keep to these rules, and one draw needn't show every extreme that they name: `pair_list`: each row names a target group and a forward group; no pair appears twice and every group is paired with itself; 80 pairs in all.
All inputs are finite; a program needn't handle non-finite values.
Results may differ from the reference program's by a relative error of at most 0.0078.
Values may be sent and summed in bfloat16 or wider, within the bound.
No kernel may reach another device: no remote copies, remote signals or barrier semaphores. Data moves between devices by JAX's collectives and lax.ppermute only.
A program may use at most 64 MiB of HBM per device.

```python
import math
import jax
import jax.numpy as jnp
from jax import lax

NC = 512
NG = 16
PLANES = 7
WAVES = 4
MODES = 64
ROWS = 8
GROUP = 4


def draw_pair_list(key, part):
    group_count = NG
    extra_count = NG * NG // 4
    quarter = max(1, NG // 4)
    key_score = jax.random.fold_in(key, 11)
    key_heavy = jax.random.fold_in(key, 12)
    scores = jax.random.randint(key_score, (group_count * group_count,), 0, 2 ** 20, dtype=jnp.int32)
    ranking = jax.random.permutation(key_heavy, group_count)
    heavy_rank = jnp.zeros((group_count,), jnp.int32).at[ranking].set(jnp.arange(group_count, dtype=jnp.int32))
    cells = jnp.arange(group_count * group_count, dtype=jnp.int32)
    target_group = cells // group_count
    forward_group = cells % group_count
    scores = scores + jnp.where(target_group == forward_group, 2 ** 30, 0).astype(jnp.int32)
    scores = scores - jnp.where(heavy_rank[forward_group] < quarter, 2 ** 19, 0).astype(jnp.int32)
    chosen = jnp.argsort(scores, stable=True)[:extra_count].astype(jnp.int32)
    extra_pairs = jnp.stack([chosen // group_count, chosen % group_count], axis=1)
    diagonal = jnp.arange(group_count, dtype=jnp.int32)
    self_pairs = jnp.stack([diagonal, diagonal], axis=1)
    return jnp.concatenate([self_pairs, extra_pairs], axis=0).astype(jnp.int32)


def plant(values, own_key, low, top_value):
    longest = values.shape.index(max(values.shape))
    spots = []
    for shift in (0, 1):
        where = [jax.random.randint(jax.random.fold_in(own_key, axis), (), 0, length) for axis, length in enumerate(values.shape)]
        where[longest] = (where[longest] + shift) % values.shape[longest]
        spots.append(tuple(where))
    return values.at[spots[0]].set(low).at[spots[1]].set(top_value)


def level_of(stream_key, extent, shards, smallest, top_value):
    level, own = 1.0, jax.random.fold_in(stream_key, 6)
    for axis_at, parts in shards:
        draws = jnp.exp(jax.random.uniform(jax.random.fold_in(own, axis_at), (parts,), jnp.float32, smallest / len(shards), top_value / len(shards)))
        level = level * jnp.repeat(draws, extent[axis_at] // parts).reshape([-1 if axis == axis_at else 1 for axis in range(len(extent))])
    return level


def bell_draw(stream_key, extent, scale, limit, split=(), kind=jnp.bfloat16):
    drawn = jax.random.normal(stream_key, extent, jnp.float32) * scale
    if len(split) > 0:
        drawn = level_of(stream_key, extent, split, -0.22, 0.18) * drawn
    return jnp.clip(drawn, min=-limit, max=limit).astype(kind)


def setup_inputs(seed: int = 0) -> dict:
    splits = jax.random.split(jax.random.key(seed), 9)
    return {
        "forward": bell_draw(splits[0], (MODES, ROWS, 2, NC), 1.0, 6.0, ((0, 8), (1, 4))),
        "backward": bell_draw(splits[1], (MODES, ROWS, 2, NC), 1.0, 6.0, ((0, 8), (1, 4))),
        "propagator": bell_draw(splits[2], (2, NC, NC), (2 * NC) ** -0.5, 0.1875),
        "row_taps": bell_draw(splits[3], (2, 3), 0.6, 3.0, (), jnp.float32),
        "phase_masks": jnp.clip(jax.random.uniform(splits[4], (PLANES, ROWS, NC), jnp.float32, -3.140625, 3.140625), -3.140625, 3.140625),
        "plane_index": plant(jax.random.randint(splits[5], (WAVES,), 0, PLANES), jax.random.fold_in(splits[5], 1), 0, PLANES - 1).astype(jnp.int32),
        "wave_ratio": jnp.clip(jnp.exp(jax.random.uniform(splits[6], (WAVES,), jnp.float32, math.log(0.7), math.log(1.4))), 0.7, 1.4),
        "pair_list": draw_pair_list(jax.random.fold_in(splits[8], 71), 0),
    }


def chosen_phases(phase_masks, plane_index, wave_ratio):
    planes = jnp.arange(phase_masks.shape[0], dtype=jnp.int32)
    selector = (plane_index[:, None] == planes[None, :]).astype(jnp.float32)
    picked = jnp.einsum('wp,prc->wrc', selector, phase_masks, precision=lax.Precision.HIGHEST)
    return picked * wave_ratio[:, None, None]

def apply_mask(forward, phases):
    mode_total, row_total, _, width = forward.shape
    wave_total = phases.shape[0]
    shaped = forward.astype(jnp.float32).reshape(mode_total // wave_total, wave_total, row_total, 2, width)
    cosine = jnp.cos(phases)[None]
    sine = jnp.sin(phases)[None]
    real_part = shaped[:, :, :, 0] * cosine - shaped[:, :, :, 1] * sine
    imag_part = shaped[:, :, :, 0] * sine + shaped[:, :, :, 1] * cosine
    return jnp.stack([real_part, imag_part], axis=3).reshape(forward.shape).astype(jnp.bfloat16)

def forward_matrix(propagator):
    top_half = jnp.concatenate([propagator[0], propagator[1]], axis=1)
    low_half = jnp.concatenate([-propagator[1], propagator[0]], axis=1)
    return jnp.concatenate([top_half, low_half], axis=0)

def backward_matrix(propagator):
    top_half = jnp.concatenate([propagator[0].T, -propagator[1].T], axis=1)
    low_half = jnp.concatenate([propagator[1].T, propagator[0].T], axis=1)
    return jnp.concatenate([top_half, low_half], axis=0)

def propagate(fields, matrix):
    width = fields.shape[-1]
    result = jnp.dot(fields.reshape(-1, 2 * width), matrix, preferred_element_type=jnp.float32)
    return result.reshape(fields.shape)

def row_stencil(padded, row_taps, adjoint):
    values = padded.astype(jnp.float32)
    below_rows = values[:, :-2]
    center = values[:, 1:-1]
    above_rows = values[:, 2:]
    tap_real = row_taps[0]
    tap_imag = row_taps[1]
    if adjoint:
        sources = (above_rows, center, below_rows)
        tap_imag = -tap_imag
    else:
        sources = (below_rows, center, above_rows)
    real_sum = jnp.zeros(center[:, :, 0].shape, jnp.float32)
    imag_sum = jnp.zeros(center[:, :, 0].shape, jnp.float32)
    for position in range(3):
        source = sources[position]
        real_sum = real_sum + tap_real[position] * source[:, :, 0] - tap_imag[position] * source[:, :, 1]
        imag_sum = imag_sum + tap_real[position] * source[:, :, 1] + tap_imag[position] * source[:, :, 0]
    return jnp.stack([real_sum, imag_sum], axis=2)

def times_i(fields):
    return jnp.stack([-fields[:, :, 1], fields[:, :, 0]], axis=2)

def times_minus_i(fields):
    return jnp.stack([fields[:, :, 1], -fields[:, :, 0]], axis=2)

def pad_rows(fields):
    return jnp.pad(fields, ((0, 0), (1, 1), (0, 0), (0, 0)))

def reference(forward, backward, propagator, row_taps, phase_masks, plane_index, wave_ratio, pair_list):
    phases = chosen_phases(phase_masks, plane_index, wave_ratio)
    masked = apply_mask(forward, phases)
    spread = propagate(masked, forward_matrix(propagator)).astype(jnp.bfloat16)
    field = row_stencil(pad_rows(spread), row_taps, False).astype(jnp.bfloat16)
    field_flat = field.reshape(MODES, -1)
    field_turned = times_minus_i(field).reshape(MODES, -1)
    target_flat = backward.reshape(MODES, -1)
    scale_pixels = 1.0 / math.sqrt(ROWS * NC)
    over_real = jnp.dot(field_flat, target_flat.T, preferred_element_type=jnp.float32) * scale_pixels
    over_imag = jnp.dot(field_turned, target_flat.T, preferred_element_type=jnp.float32) * scale_pixels
    group_ids = jnp.arange(NG, dtype=jnp.int32)
    hits = (pair_list[:, 0][:, None, None] == group_ids[None, :, None]) & (pair_list[:, 1][:, None, None] == group_ids[None, None, :])
    pair_matrix = lax.optimization_barrier(jnp.sum(hits.astype(jnp.float32), axis=0))
    mode_groups = jnp.arange(MODES, dtype=jnp.int32) // GROUP
    full_mask = pair_matrix[mode_groups][:, mode_groups]
    coupling = jnp.stack([over_real * full_mask.T, over_imag * full_mask.T])
    weights = coupling.astype(jnp.bfloat16)
    target_turned = times_i(backward).reshape(MODES, -1)
    gathered = jnp.dot(weights[0], target_flat, preferred_element_type=jnp.float32)
    gathered = gathered + jnp.dot(weights[1], target_turned, preferred_element_type=jnp.float32)
    gathered = (gathered * (1.0 / math.sqrt(MODES))).astype(jnp.bfloat16).reshape(forward.shape)
    pulled = row_stencil(pad_rows(gathered), row_taps, True).astype(jnp.bfloat16)
    adjoint = propagate(pulled, backward_matrix(propagator))
    masked_float = masked.astype(jnp.float32)
    term = masked_float[:, :, 1] * adjoint[:, :, 0] - masked_float[:, :, 0] * adjoint[:, :, 1]
    summed = lax.optimization_barrier(jnp.sum(term.reshape(MODES // WAVES, WAVES, ROWS, NC), axis=0))
    mask_grad = summed * (-2.0 / math.sqrt(MODES))
    return (coupling, mask_grad)
```

```python
import math

import jax
import jax.numpy as jnp
from jax import lax
from jax.experimental import pallas as pl
from jax.experimental.pallas import tpu as pltpu
from jax.sharding import PartitionSpec as P

NG = 16
VMEM_BYTES = 24 << 20
NT = (((1,), (1,)), ((), ()))
F32 = jnp.float32
BF16 = jnp.bfloat16


def size_of(item):
    return math.prod(item.shape) * jnp.dtype(item.dtype).itemsize


def local_call(fn, outs, arrays, scalars=(), flops=0):
    moved = sum(size_of(item) for item in (*arrays, *outs))
    if moved > VMEM_BYTES:
        return fn(*scalars, *arrays)
    first = len(scalars)
    count = first + len(arrays)

    def kernel(*refs):
        values = fn(*refs[:first], *[ref[...] for ref in refs[first:count]])
        for ref, value in zip(refs[count:], values):
            ref[...] = value

    return pl.pallas_call(
        kernel,
        out_shape=tuple(outs),
        in_specs=[pl.BlockSpec(memory_space=pltpu.SMEM)] * first
        + [pl.BlockSpec(memory_space=pltpu.VMEM)] * len(arrays),
        out_specs=tuple(pl.BlockSpec(memory_space=pltpu.VMEM) for _ in outs),
        cost_estimate=pl.CostEstimate(flops=flops, bytes_accessed=moved, transcendentals=0),
        compiler_params=pltpu.CompilerParams(vmem_limit_bytes=48 << 20),
    )(*scalars, *arrays)


def array(shape, dtype):
    return jax.ShapeDtypeStruct(shape, dtype)


def swapped(values, axis, distance):
    peers = lax.axis_size(axis)
    return lax.ppermute(values, axis, [(i, i ^ distance) for i in range(peers)])


def neighbour_rows(fields):
    peers = lax.axis_size("row")
    odd = lax.axis_index("row") % 2 == 1
    modes = fields.shape[0]
    first = fields[:, 0].reshape(modes, -1)
    last = fields[:, -1].reshape(modes, -1)
    even_pairs = [(i, i + 1) for i in range(0, peers - 1, 2)]
    odd_pairs = [(i, i + 1) for i in range(1, peers - 1, 2)]
    both_ways = lambda pairs: pairs + [(j, i) for i, j in pairs]
    over_odd = lax.ppermute(jnp.where(odd, last, first), "row", both_ways(odd_pairs))
    over_even = lax.ppermute(jnp.where(odd, first, last), "row", both_ways(even_pairs))
    return jnp.where(odd, over_even, over_odd), jnp.where(odd, over_odd, over_even)


def rounds_of(peers):
    bits = [1 << k for k in reversed(range(peers.bit_length() - 1))]
    head, tail = bits[:-2], bits[-2:]
    last = [tail[0], tail[1], tail[0] ^ tail[1]] if len(tail) == 2 else tail
    return head, last


def pulled_rows(rows, width):
    def fn(taps, own, before, after):
        half = rows * width
        real = [before[:, :width]] + [own[:, j * width : (j + 1) * width] for j in range(rows)]
        imag = [before[:, width:]] + [
            own[:, half + j * width : half + (j + 1) * width] for j in range(rows)
        ]
        real = [part.astype(F32) for part in real + [after[:, :width]]]
        imag = [part.astype(F32) for part in imag + [after[:, width:]]]
        out_real, out_imag = [], []
        for j in range(1, rows + 1):
            sources = (j + 1, j, j - 1)
            total_real = total_imag = 0.0
            for k in range(3):
                a, b = taps[0, k], taps[1, k]
                total_real = total_real + a * real[sources[k]] + b * imag[sources[k]]
                total_imag = total_imag + a * imag[sources[k]] - b * real[sources[k]]
            out_real.append(total_real)
            out_imag.append(total_imag)
        return (jnp.concatenate(out_real + out_imag, axis=1).astype(BF16),)

    return fn


def halves(pieces):
    whole = jnp.concatenate(pieces, axis=0) if len(pieces) > 1 else pieces[0]
    half = whole.shape[1] // 2
    return whole[:, :half], whole[:, half:]


def by_rows(values, width):
    return [values[:, at : at + width] for at in range(0, values.shape[1], width)]


def spread_all(width):
    def fn(cosine, sine, propagator, *pieces):
        real, imag = halves(pieces)
        total, half = real.shape
        shape = (total // cosine.shape[0], *cosine.shape)
        real = real.astype(F32).reshape(shape)
        imag = imag.astype(F32).reshape(shape)
        masked_real = (real * cosine - imag * sine).reshape(total, half).astype(BF16)
        masked_imag = (real * sine + imag * cosine).reshape(total, half).astype(BF16)
        masked = jnp.concatenate([masked_real, masked_imag], axis=0)
        stacked = jnp.concatenate(by_rows(masked, width), axis=0)
        over_real = jnp.dot(stacked, propagator[0], preferred_element_type=F32)
        over_imag = jnp.dot(stacked, propagator[1], preferred_element_type=F32)
        out_real, out_imag = [], []
        for at in range(0, stacked.shape[0], 2 * total):
            first, second = slice(at, at + total), slice(at + total, at + 2 * total)
            out_real.append(over_real[first] - over_imag[second])
            out_imag.append(over_imag[first] + over_real[second])
        spread = jnp.concatenate(
            [jnp.concatenate(out_real, axis=1), jnp.concatenate(out_imag, axis=1)], axis=0
        )
        return masked, spread.astype(BF16)

    return fn


def project(spread, *pieces):
    targets = jnp.concatenate(halves(pieces), axis=0)
    total = targets.shape[0] // 2
    product = lax.dot_general(spread, targets, NT, preferred_element_type=F32)
    real = product[:total, :total] + product[total:, total:]
    imag = product[total:, :total] - product[:total, total:]
    return (jnp.concatenate([real, imag], axis=1),)


def back_propagated(width):
    def fn(propagator, *pieces):
        targets = jnp.concatenate(halves(pieces), axis=0)
        total = targets.shape[0] // 2
        stacked = jnp.concatenate(by_rows(targets, width), axis=0)
        over_real = lax.dot_general(stacked, propagator[0], NT, preferred_element_type=F32)
        over_imag = lax.dot_general(stacked, propagator[1], NT, preferred_element_type=F32)
        out_real, out_imag = [], []
        for at in range(0, stacked.shape[0], 2 * total):
            first, second = slice(at, at + total), slice(at + total, at + 2 * total)
            out_real.append(over_real[first] + over_imag[second])
            out_imag.append(over_real[second] - over_imag[first])
        result = jnp.concatenate(
            [jnp.concatenate(out_real, axis=1), jnp.concatenate(out_imag, axis=1)], axis=0
        )
        return (result.astype(BF16),)

    return fn


def finish(local_modes, waves, rows, width, scale_pixels, scale_grad):
    def fn(mask, order, back, masked, *partials):
        total = mask.shape[0]
        summed = partials[0]
        for part in partials[1:]:
            summed = summed + part
        real = summed[:, :total] * scale_pixels * mask
        imag = summed[:, total:] * scale_pixels * mask
        own = jnp.concatenate([real[:local_modes], imag[:local_modes]], axis=0)
        own = jnp.dot(own, order, precision=lax.Precision.HIGHEST, preferred_element_type=F32)
        coupling = own.reshape(2, local_modes, total)
        weight_real, weight_imag = real.astype(BF16), imag.astype(BF16)
        weights = jnp.concatenate(
            [
                jnp.concatenate([weight_real, -weight_imag], axis=1),
                jnp.concatenate([weight_imag, weight_real], axis=1),
            ],
            axis=0,
        )
        adjoint = jnp.dot(weights, back, preferred_element_type=F32)
        fields = masked.astype(F32)
        term = fields[total:] * adjoint[:total] - fields[:total] * adjoint[total:]
        group = 2 * waves
        folded = jnp.sum(term.reshape(total // group, group, rows * width), axis=0)
        folded = (folded[:waves] + folded[waves:]) * scale_grad
        grad = jnp.stack(by_rows(folded, width), axis=1)
        return coupling, grad

    return fn


def body(forward, backward, propagator, row_taps, phase_masks, plane_index, wave_ratio, pair_list):
    local_modes, rows, _, width = forward.shape
    waves = wave_ratio.shape[0]
    mode_peers = lax.axis_size("mode")
    row_peers = lax.axis_size("row")
    total = local_modes * mode_peers
    row_total = rows * row_peers
    group_size = total // NG
    half = rows * width

    flat = lambda fields: fields.transpose(0, 2, 1, 3).reshape(local_modes, 2 * half)
    own_forward, own_backward = flat(forward), flat(backward)

    before, after = neighbour_rows(backward)
    (own_pulled,) = local_call(
        pulled_rows(rows, width),
        [array((local_modes, 2 * half), BF16)],
        [own_backward, before, after],
        [row_taps],
        flops=24 * local_modes * half,
    )

    head, last = rounds_of(mode_peers)
    keys = [0]
    fields, targets = own_forward, own_pulled
    for distance in head:
        fields = jnp.concatenate([fields, swapped(fields, "mode", distance)], axis=0)
        targets = jnp.concatenate([targets, swapped(targets, "mode", distance)], axis=0)
        keys = keys + [key ^ distance for key in keys]
    field_pieces = [fields] + [swapped(fields, "mode", distance) for distance in last]
    target_pieces = [targets] + [swapped(targets, "mode", distance) for distance in last]
    keys = keys + [key ^ distance for distance in last for key in keys]

    planes = jnp.arange(phase_masks.shape[0], dtype=jnp.int32)
    selector = (plane_index[:, None] == planes[None, :]).astype(F32)
    picked = jnp.einsum("wp,prc->wrc", selector, phase_masks, precision=lax.Precision.HIGHEST)
    phases = (picked * wave_ratio[:, None, None]).reshape(waves, half)
    cosine = jnp.tile(jnp.cos(phases), (2, 1))
    sine = jnp.tile(jnp.sin(phases), (2, 1))

    peers = jnp.asarray(keys, jnp.int32) ^ lax.axis_index("mode").astype(jnp.int32)
    lanes = jnp.arange(local_modes, dtype=jnp.int32)
    numbers = (peers[:, None] * local_modes + lanes[None, :]).reshape(total)
    groups = numbers // group_size
    to_target = (pair_list[:, 0][:, None] == groups[None, :]).astype(BF16)
    to_forward = (pair_list[:, 1][:, None] == groups[None, :]).astype(BF16)
    mask = lax.dot_general(
        to_forward, to_target, (((0,), (0,)), ((), ())), preferred_element_type=F32
    )
    order = (numbers[:, None] == jnp.arange(total, dtype=jnp.int32)[None, :]).astype(F32)

    masked, spread = local_call(
        spread_all(width),
        [array((2 * total, half), BF16)] * 2,
        [cosine, sine, propagator, *field_pieces],
        flops=8 * total * half * width,
    )
    (partial,) = local_call(
        project,
        [array((total, 2 * total), F32)],
        [spread, *target_pieces],
        flops=8 * total * total * half,
    )
    partials = [partial] + [swapped(partial, "row", d) for d in range(row_peers - 1, 0, -1)]
    (back,) = local_call(
        back_propagated(width),
        [array((2 * total, half), BF16)],
        [propagator, *target_pieces],
        flops=8 * total * half * width,
    )
    coupling, mask_grad = local_call(
        finish(
            local_modes,
            waves,
            rows,
            width,
            1.0 / math.sqrt(row_total * width),
            -2.0 / total,
        ),
        [array((2, local_modes, total), F32), array((waves, rows, width), F32)],
        [mask, order, back, masked, *partials],
        flops=8 * total * total * half,
    )
    return coupling, mask_grad


def solution(mesh):
    in_specs = (
        P("mode", "row", None, None),
        P("mode", "row", None, None),
        P(),
        P(),
        P(None, "row", None),
        P(),
        P(),
        P(),
    )
    out_specs = (P(None, "mode", None), P(None, "row", None))
    return jax.shard_map(body, mesh=mesh, in_specs=in_specs, out_specs=out_specs, check_vma=False)
```

```python
import math

import jax
import jax.numpy as jnp
from jax import lax
from jax.experimental import pallas as pl
from jax.experimental.pallas import tpu as pltpu
from jax.sharding import PartitionSpec as P

NG = 16
VMEM_BYTES = 24 << 20
NT = (((1,), (1,)), ((), ()))
F32 = jnp.float32
BF16 = jnp.bfloat16


def size_of(item):
    return math.prod(item.shape) * jnp.dtype(item.dtype).itemsize


def local_call(fn, outs, arrays, flops=0):
    moved = sum(size_of(item) for item in (*arrays, *outs))
    if moved > VMEM_BYTES:
        return fn(*arrays)
    count = len(arrays)

    def kernel(*refs):
        values = fn(*[ref[...] for ref in refs[:count]])
        for ref, value in zip(refs[count:], values):
            ref[...] = value

    return pl.pallas_call(
        kernel,
        out_shape=tuple(outs),
        in_specs=[pl.BlockSpec(memory_space=pltpu.VMEM)] * count,
        out_specs=tuple(pl.BlockSpec(memory_space=pltpu.VMEM) for _ in outs),
        cost_estimate=pl.CostEstimate(flops=flops, bytes_accessed=moved, transcendentals=0),
        compiler_params=pltpu.CompilerParams(vmem_limit_bytes=48 << 20),
    )(*arrays)


def array(shape, dtype):
    return jax.ShapeDtypeStruct(shape, dtype)


def swapped(values, axis, distance):
    peers = lax.axis_size(axis)
    return lax.ppermute(values, axis, [(i, i ^ distance) for i in range(peers)])


def neighbour_rows(fields):
    peers = lax.axis_size("row")
    odd = lax.axis_index("row") % 2 == 1
    modes = fields.shape[0]
    even_pairs = [(i, i + 1) for i in range(0, peers - 1, 2)]
    odd_pairs = [(i, i + 1) for i in range(1, peers - 1, 2)]
    both_ways = lambda pairs: pairs + [(j, i) for i, j in pairs]
    over_odd = lax.ppermute(fields, "row", both_ways(odd_pairs))
    over_even = lax.ppermute(fields, "row", both_ways(even_pairs))
    before = jnp.where(odd, over_even[:, -1], over_odd[:, -1])
    after = jnp.where(odd, over_odd[:, 0], over_even[:, 0])
    return before.reshape(modes, -1), after.reshape(modes, -1)


def rounds_of(peers):
    bits = [1 << k for k in reversed(range(peers.bit_length() - 1))]
    head, tail = bits[:-2], bits[-2:]
    last = [tail[0], tail[1], tail[0] ^ tail[1]] if len(tail) == 2 else tail
    return head, last


def pulled_rows(rows, width):
    def fn(taps, own, before, after):
        half = rows * width
        real = [before[:, :width]] + [own[:, j * width : (j + 1) * width] for j in range(rows)]
        imag = [before[:, width:]] + [
            own[:, half + j * width : half + (j + 1) * width] for j in range(rows)
        ]
        real = [part.astype(F32) for part in real + [after[:, :width]]]
        imag = [part.astype(F32) for part in imag + [after[:, width:]]]
        out_real, out_imag = [], []
        for j in range(1, rows + 1):
            sources = (j + 1, j, j - 1)
            total_real = total_imag = 0.0
            for k in range(3):
                a, b = taps[0:1, k : k + 1], taps[1:2, k : k + 1]
                total_real = total_real + a * real[sources[k]] + b * imag[sources[k]]
                total_imag = total_imag + a * imag[sources[k]] - b * real[sources[k]]
            out_real.append(total_real)
            out_imag.append(total_imag)
        return (jnp.concatenate(out_real + out_imag, axis=1).astype(BF16),)

    return fn


def halves(pieces):
    whole = jnp.concatenate(pieces, axis=0) if len(pieces) > 1 else pieces[0]
    half = whole.shape[1] // 2
    return whole[:, :half], whole[:, half:]


def by_rows(values, width):
    return [values[:, at : at + width] for at in range(0, values.shape[1], width)]


def spread_all(width):
    def fn(cosine, sine, propagator, *pieces):
        real, imag = halves(pieces)
        total, half = real.shape
        shape = (total // cosine.shape[0], *cosine.shape)
        real = real.astype(F32).reshape(shape)
        imag = imag.astype(F32).reshape(shape)
        masked_real = (real * cosine - imag * sine).reshape(total, half).astype(BF16)
        masked_imag = (real * sine + imag * cosine).reshape(total, half).astype(BF16)
        masked = jnp.concatenate([masked_real, masked_imag], axis=0)
        stacked = jnp.concatenate(by_rows(masked, width), axis=0)
        over_real = jnp.dot(stacked, propagator[0], preferred_element_type=F32)
        over_imag = jnp.dot(stacked, propagator[1], preferred_element_type=F32)
        out_real, out_imag = [], []
        for at in range(0, stacked.shape[0], 2 * total):
            first, second = slice(at, at + total), slice(at + total, at + 2 * total)
            out_real.append(over_real[first] - over_imag[second])
            out_imag.append(over_imag[first] + over_real[second])
        spread = jnp.concatenate(
            [jnp.concatenate(out_real, axis=1), jnp.concatenate(out_imag, axis=1)], axis=0
        )
        return masked, spread.astype(BF16)

    return fn


def project(spread, *pieces):
    targets = jnp.concatenate(halves(pieces), axis=0)
    total = targets.shape[0] // 2
    product = lax.dot_general(spread, targets, NT, preferred_element_type=F32)
    real = product[:total, :total] + product[total:, total:]
    imag = product[total:, :total] - product[:total, total:]
    return (jnp.concatenate([real, imag], axis=1),)


def back_propagated(width):
    def fn(propagator, *pieces):
        targets = jnp.concatenate(halves(pieces), axis=0)
        total = targets.shape[0] // 2
        stacked = jnp.concatenate(by_rows(targets, width), axis=0)
        over_real = lax.dot_general(stacked, propagator[0], NT, preferred_element_type=F32)
        over_imag = lax.dot_general(stacked, propagator[1], NT, preferred_element_type=F32)
        out_real, out_imag = [], []
        for at in range(0, stacked.shape[0], 2 * total):
            first, second = slice(at, at + total), slice(at + total, at + 2 * total)
            out_real.append(over_real[first] + over_imag[second])
            out_imag.append(over_real[second] - over_imag[first])
        result = jnp.concatenate(
            [jnp.concatenate(out_real, axis=1), jnp.concatenate(out_imag, axis=1)], axis=0
        )
        return (result.astype(BF16),)

    return fn


def finish(local_modes, waves, rows, width, scale_pixels, scale_grad):
    def fn(mask, order, back, masked, *partials):
        total = mask.shape[0]
        summed = partials[0]
        for part in partials[1:]:
            summed = summed + part
        real = summed[:, :total] * scale_pixels * mask
        imag = summed[:, total:] * scale_pixels * mask
        own = jnp.concatenate([real[:local_modes], imag[:local_modes]], axis=0)
        own = jnp.dot(own, order, precision=lax.Precision.HIGHEST, preferred_element_type=F32)
        coupling = own.reshape(2, local_modes, total)
        weight_real, weight_imag = real.astype(BF16), imag.astype(BF16)
        weights = jnp.concatenate(
            [
                jnp.concatenate([weight_real, -weight_imag], axis=1),
                jnp.concatenate([weight_imag, weight_real], axis=1),
            ],
            axis=0,
        )
        adjoint = jnp.dot(weights, back, preferred_element_type=F32)
        fields = masked.astype(F32)
        term = fields[total:] * adjoint[:total] - fields[:total] * adjoint[total:]
        group = 2 * waves
        folded = jnp.sum(term.reshape(total // group, group, rows * width), axis=0)
        folded = (folded[:waves] + folded[waves:]) * scale_grad
        grad = jnp.stack(by_rows(folded, width), axis=1)
        return coupling, grad

    return fn


def body(forward, backward, propagator, row_taps, phase_masks, plane_index, wave_ratio, pair_list):
    local_modes, rows, _, width = forward.shape
    waves = wave_ratio.shape[0]
    mode_peers = lax.axis_size("mode")
    row_peers = lax.axis_size("row")
    total = local_modes * mode_peers
    row_total = rows * row_peers
    group_size = total // NG
    half = rows * width

    flat = lambda fields: fields.transpose(0, 2, 1, 3).reshape(local_modes, 2 * half)
    own_backward = flat(backward)
    before, after = neighbour_rows(backward)
    (own_pulled,) = local_call(
        pulled_rows(rows, width),
        [array((local_modes, 2 * half), BF16)],
        [jnp.pad(row_taps, ((0, 6), (0, 125))), own_backward, before, after],
        flops=24 * local_modes * half,
    )

    head, last = rounds_of(mode_peers)
    distances = head + last[:2]
    fields, targets = forward, own_pulled
    for distance in head:
        received = swapped(fields, "mode", distance)
        if fields.ndim > 2:
            fields, received = flat(fields), flat(received)
        fields = jnp.concatenate([fields, received], axis=0)
        targets = jnp.concatenate([targets, swapped(targets, "mode", distance)], axis=0)
    if fields.ndim > 2:
        fields = flat(fields)
    targets, pair_list, plane_index, wave_ratio, phase_masks = lax.optimization_barrier(
        (targets, pair_list, plane_index, wave_ratio, phase_masks)
    )
    field_pieces = [fields] + [swapped(fields, "mode", distance) for distance in last]
    target_pieces = [targets] + [swapped(targets, "mode", distance) for distance in last]

    planes = jnp.arange(phase_masks.shape[0], dtype=jnp.int32)
    selector = (plane_index[:, None] == planes[None, :]).astype(F32)
    picked = jnp.einsum("wp,prc->wrc", selector, phase_masks, precision=lax.Precision.HIGHEST)
    phases = (picked * wave_ratio[:, None, None]).reshape(waves, half)
    cosine = jnp.tile(jnp.cos(phases), (2, 1))
    sine = jnp.tile(jnp.sin(phases), (2, 1))

    places = jnp.arange(total, dtype=jnp.int32)
    peers = lax.axis_index("mode").astype(jnp.int32)
    for k, distance in enumerate(distances):
        peers = peers ^ ((places // (local_modes << k)) % 2 * distance)
    numbers = peers * local_modes + places % local_modes
    groups = numbers // group_size
    to_target = (pair_list[:, 0][:, None] == groups[None, :]).astype(BF16)
    to_forward = (pair_list[:, 1][:, None] == groups[None, :]).astype(BF16)
    mask = lax.dot_general(
        to_forward, to_target, (((0,), (0,)), ((), ())), preferred_element_type=F32
    )
    order = (numbers[:, None] == places[None, :]).astype(F32)

    masked, spread = local_call(
        spread_all(width),
        [array((2 * total, half), BF16)] * 2,
        [cosine, sine, propagator, *field_pieces],
        flops=8 * total * half * width,
    )
    (partial,) = local_call(
        project,
        [array((total, 2 * total), F32)],
        [spread, *target_pieces],
        flops=8 * total * total * half,
    )
    partials = [partial] + [swapped(partial, "row", d) for d in range(row_peers - 1, 0, -1)]
    (back,) = local_call(
        back_propagated(width),
        [array((2 * total, half), BF16)],
        [propagator, *target_pieces],
        flops=8 * total * half * width,
    )
    coupling, mask_grad = local_call(
        finish(
            local_modes,
            waves,
            rows,
            width,
            1.0 / math.sqrt(row_total * width),
            -2.0 / total,
        ),
        [array((2, local_modes, total), F32), array((waves, rows, width), F32)],
        [mask, order, back, masked, *partials],
        flops=8 * total * total * half,
    )
    return coupling, mask_grad


def solution(mesh):
    in_specs = (
        P("mode", "row", None, None),
        P("mode", "row", None, None),
        P(),
        P(),
        P(None, "row", None),
        P(),
        P(),
        P(),
    )
    out_specs = (P(None, "mode", None), P(None, "row", None))
    return jax.shard_map(body, mesh=mesh, in_specs=in_specs, out_specs=out_specs, check_vma=False)
```

```python
import math

import jax
import jax.numpy as jnp
from jax import lax
from jax.experimental import pallas as pl
from jax.experimental.pallas import tpu as pltpu
from jax.sharding import PartitionSpec as P

NG = 16
VMEM_BYTES = 24 << 20
NT = (((1,), (1,)), ((), ()))
F32 = jnp.float32
BF16 = jnp.bfloat16


def size_of(item):
    return math.prod(item.shape) * jnp.dtype(item.dtype).itemsize


def local_call(fn, outs, arrays, flops=0):
    moved = sum(size_of(item) for item in (*arrays, *outs))
    if moved > VMEM_BYTES:
        return fn(*arrays)
    count = len(arrays)

    def kernel(*refs):
        values = fn(*[ref[...] for ref in refs[:count]])
        for ref, value in zip(refs[count:], values):
            ref[...] = value

    return pl.pallas_call(
        kernel,
        out_shape=tuple(outs),
        in_specs=[pl.BlockSpec(memory_space=pltpu.VMEM)] * count,
        out_specs=tuple(pl.BlockSpec(memory_space=pltpu.VMEM) for _ in outs),
        cost_estimate=pl.CostEstimate(flops=flops, bytes_accessed=moved, transcendentals=0),
        compiler_params=pltpu.CompilerParams(vmem_limit_bytes=48 << 20),
    )(*arrays)


def array(shape, dtype):
    return jax.ShapeDtypeStruct(shape, dtype)


def swapped(values, axis, distance):
    peers = lax.axis_size(axis)
    return lax.ppermute(values, axis, [(i, i ^ distance) for i in range(peers)])


def neighbour_rows(fields):
    peers = lax.axis_size("row")
    odd = lax.axis_index("row") % 2 == 1
    modes = fields.shape[0]
    even_pairs = [(i, i + 1) for i in range(0, peers - 1, 2)]
    odd_pairs = [(i, i + 1) for i in range(1, peers - 1, 2)]
    both_ways = lambda pairs: pairs + [(j, i) for i, j in pairs]
    over_odd = lax.ppermute(fields, "row", both_ways(odd_pairs))
    over_even = lax.ppermute(fields, "row", both_ways(even_pairs))
    before = jnp.where(odd, over_even[:, -1], over_odd[:, -1])
    after = jnp.where(odd, over_odd[:, 0], over_even[:, 0])
    return before.reshape(modes, -1), after.reshape(modes, -1)


def rounds_of(peers):
    bits = [1 << k for k in reversed(range(peers.bit_length() - 1))]
    head, tail = bits[:-2], bits[-2:]
    last = [tail[0], tail[1], tail[0] ^ tail[1]] if len(tail) == 2 else tail
    return head, last


def gathered_last(values, last):
    pieces = [swapped(values, "mode", distance) for distance in reversed(last)]
    return [values] + pieces[::-1]


def pulled_rows(rows, width):
    def fn(taps, own, before, after):
        half = rows * width
        real = [before[:, :width]] + [own[:, j * width : (j + 1) * width] for j in range(rows)]
        imag = [before[:, width:]] + [
            own[:, half + j * width : half + (j + 1) * width] for j in range(rows)
        ]
        real = [part.astype(F32) for part in real + [after[:, :width]]]
        imag = [part.astype(F32) for part in imag + [after[:, width:]]]
        out_real, out_imag = [], []
        for j in range(1, rows + 1):
            sources = (j + 1, j, j - 1)
            total_real = total_imag = 0.0
            for k in range(3):
                a, b = taps[0:1, k : k + 1], taps[1:2, k : k + 1]
                total_real = total_real + a * real[sources[k]] + b * imag[sources[k]]
                total_imag = total_imag + a * imag[sources[k]] - b * real[sources[k]]
            out_real.append(total_real)
            out_imag.append(total_imag)
        return (jnp.concatenate(out_real + out_imag, axis=1).astype(BF16),)

    return fn


def halves(pieces):
    whole = jnp.concatenate(pieces, axis=0) if len(pieces) > 1 else pieces[0]
    half = whole.shape[1] // 2
    return whole[:, :half], whole[:, half:]


def by_rows(values, width):
    return [values[:, at : at + width] for at in range(0, values.shape[1], width)]


def spread_all(width):
    def fn(cosine, sine, propagator, *pieces):
        real, imag = halves(pieces)
        total, half = real.shape
        shape = (total // cosine.shape[0], *cosine.shape)
        real = real.astype(F32).reshape(shape)
        imag = imag.astype(F32).reshape(shape)
        masked_real = (real * cosine - imag * sine).reshape(total, half).astype(BF16)
        masked_imag = (real * sine + imag * cosine).reshape(total, half).astype(BF16)
        masked = jnp.concatenate([masked_real, masked_imag], axis=0)
        stacked = jnp.concatenate(by_rows(masked, width), axis=0)
        over_real = jnp.dot(stacked, propagator[0], preferred_element_type=F32)
        over_imag = jnp.dot(stacked, propagator[1], preferred_element_type=F32)
        out_real, out_imag = [], []
        for at in range(0, stacked.shape[0], 2 * total):
            first, second = slice(at, at + total), slice(at + total, at + 2 * total)
            out_real.append(over_real[first] - over_imag[second])
            out_imag.append(over_imag[first] + over_real[second])
        spread = jnp.concatenate(
            [jnp.concatenate(out_real, axis=1), jnp.concatenate(out_imag, axis=1)], axis=0
        )
        return masked, spread.astype(BF16)

    return fn


def project(spread, *pieces):
    targets = jnp.concatenate(halves(pieces), axis=0)
    total = targets.shape[0] // 2
    product = lax.dot_general(spread, targets, NT, preferred_element_type=F32)
    real = product[:total, :total] + product[total:, total:]
    imag = product[total:, :total] - product[:total, total:]
    return (jnp.concatenate([real, imag], axis=1),)


def back_propagated(width):
    def fn(propagator, *pieces):
        targets = jnp.concatenate(halves(pieces), axis=0)
        total = targets.shape[0] // 2
        stacked = jnp.concatenate(by_rows(targets, width), axis=0)
        over_real = lax.dot_general(stacked, propagator[0], NT, preferred_element_type=F32)
        over_imag = lax.dot_general(stacked, propagator[1], NT, preferred_element_type=F32)
        out_real, out_imag = [], []
        for at in range(0, stacked.shape[0], 2 * total):
            first, second = slice(at, at + total), slice(at + total, at + 2 * total)
            out_real.append(over_real[first] + over_imag[second])
            out_imag.append(over_real[second] - over_imag[first])
        result = jnp.concatenate(
            [jnp.concatenate(out_real, axis=1), jnp.concatenate(out_imag, axis=1)], axis=0
        )
        return (result.astype(BF16),)

    return fn


def finish(local_modes, waves, rows, width, scale_pixels, scale_grad):
    def fn(mask, order, back, masked, *partials):
        total = mask.shape[0]
        summed = partials[0]
        for part in partials[1:]:
            summed = summed + part
        real = summed[:, :total] * scale_pixels * mask
        imag = summed[:, total:] * scale_pixels * mask
        own = jnp.concatenate([real[:local_modes], imag[:local_modes]], axis=0)
        own = jnp.dot(own, order, precision=lax.Precision.HIGHEST, preferred_element_type=F32)
        coupling = own.reshape(2, local_modes, total)
        weight_real, weight_imag = real.astype(BF16), imag.astype(BF16)
        weights = jnp.concatenate(
            [
                jnp.concatenate([weight_real, -weight_imag], axis=1),
                jnp.concatenate([weight_imag, weight_real], axis=1),
            ],
            axis=0,
        )
        adjoint = jnp.dot(weights, back, preferred_element_type=F32)
        fields = masked.astype(F32)
        term = fields[total:] * adjoint[:total] - fields[:total] * adjoint[total:]
        group = 2 * waves
        folded = jnp.sum(term.reshape(total // group, group, rows * width), axis=0)
        folded = (folded[:waves] + folded[waves:]) * scale_grad
        grad = jnp.stack(by_rows(folded, width), axis=1)
        return coupling, grad

    return fn


def body(forward, backward, propagator, row_taps, phase_masks, plane_index, wave_ratio, pair_list):
    local_modes, rows, _, width = forward.shape
    waves = wave_ratio.shape[0]
    mode_peers = lax.axis_size("mode")
    row_peers = lax.axis_size("row")
    total = local_modes * mode_peers
    row_total = rows * row_peers
    group_size = total // NG
    half = rows * width

    flat = lambda fields: fields.transpose(0, 2, 1, 3).reshape(local_modes, 2 * half)
    own_backward = flat(backward)
    before, after = neighbour_rows(backward)
    (own_pulled,) = local_call(
        pulled_rows(rows, width),
        [array((local_modes, 2 * half), BF16)],
        [jnp.pad(row_taps, ((0, 6), (0, 125))), own_backward, before, after],
        flops=24 * local_modes * half,
    )

    head, last = rounds_of(mode_peers)
    distances = head + last[:2]
    both = jnp.concatenate([flat(forward), own_pulled], axis=1)
    fields = jnp.zeros((1, 1))
    targets = both
    for distance in head:
        targets = jnp.concatenate([targets, swapped(targets, "mode", distance)], axis=0)
    if fields.ndim > 2:
        fields = flat(fields)
    targets, pair_list, plane_index, wave_ratio, phase_masks = lax.optimization_barrier(
        (targets, pair_list, plane_index, wave_ratio, phase_masks)
    )
    pieces = gathered_last(targets, last)
    field_pieces = [p[:, : 2 * half] for p in pieces]
    target_pieces = [p[:, 2 * half :] for p in pieces]

    planes = jnp.arange(phase_masks.shape[0], dtype=jnp.int32)
    selector = (plane_index[:, None] == planes[None, :]).astype(F32)
    picked = jnp.einsum("wp,prc->wrc", selector, phase_masks, precision=lax.Precision.HIGHEST)
    phases = (picked * wave_ratio[:, None, None]).reshape(waves, half)
    cosine = jnp.tile(jnp.cos(phases), (2, 1))
    sine = jnp.tile(jnp.sin(phases), (2, 1))

    places = jnp.arange(total, dtype=jnp.int32)
    peers = lax.axis_index("mode").astype(jnp.int32)
    for k, distance in enumerate(distances):
        peers = peers ^ ((places // (local_modes << k)) % 2 * distance)
    numbers = peers * local_modes + places % local_modes
    groups = numbers // group_size
    to_target = (pair_list[:, 0][:, None] == groups[None, :]).astype(BF16)
    to_forward = (pair_list[:, 1][:, None] == groups[None, :]).astype(BF16)
    mask = lax.dot_general(
        to_forward, to_target, (((0,), (0,)), ((), ())), preferred_element_type=F32
    )
    order = (numbers[:, None] == places[None, :]).astype(F32)

    masked, spread = local_call(
        spread_all(width),
        [array((2 * total, half), BF16)] * 2,
        [cosine, sine, propagator, *field_pieces],
        flops=8 * total * half * width,
    )
    (partial,) = local_call(
        project,
        [array((total, 2 * total), F32)],
        [spread, *target_pieces],
        flops=8 * total * total * half,
    )
    partials = [partial] + [swapped(partial, "row", d) for d in range(row_peers - 1, 0, -1)]
    (back,) = local_call(
        back_propagated(width),
        [array((2 * total, half), BF16)],
        [propagator, *target_pieces],
        flops=8 * total * half * width,
    )
    coupling, mask_grad = local_call(
        finish(
            local_modes,
            waves,
            rows,
            width,
            1.0 / math.sqrt(row_total * width),
            -2.0 / total,
        ),
        [array((2, local_modes, total), F32), array((waves, rows, width), F32)],
        [mask, order, back, masked, *partials],
        flops=8 * total * total * half,
    )
    return coupling, mask_grad


def solution(mesh):
    in_specs = (
        P("mode", "row", None, None),
        P("mode", "row", None, None),
        P(),
        P(),
        P(None, "row", None),
        P(),
        P(),
        P(),
    )
    out_specs = (P(None, "mode", None), P(None, "row", None))
    return jax.shard_map(body, mesh=mesh, in_specs=in_specs, out_specs=out_specs, check_vma=False)
```

```python
import math

import jax
import jax.numpy as jnp
from jax import lax
from jax.experimental import pallas as pl
from jax.experimental.pallas import tpu as pltpu
from jax.sharding import PartitionSpec as P

NG = 16
VMEM_BYTES = 24 << 20
NT = (((1,), (1,)), ((), ()))
F32 = jnp.float32
BF16 = jnp.bfloat16


def size_of(item):
    return math.prod(item.shape) * jnp.dtype(item.dtype).itemsize


def local_call(fn, outs, arrays, flops=0):
    moved = sum(size_of(item) for item in (*arrays, *outs))
    if moved > VMEM_BYTES:
        return fn(*arrays)
    count = len(arrays)

    def kernel(*refs):
        values = fn(*[ref[...] for ref in refs[:count]])
        for ref, value in zip(refs[count:], values):
            ref[...] = value

    return pl.pallas_call(
        kernel,
        out_shape=tuple(outs),
        in_specs=[pl.BlockSpec(memory_space=pltpu.VMEM)] * count,
        out_specs=tuple(pl.BlockSpec(memory_space=pltpu.VMEM) for _ in outs),
        cost_estimate=pl.CostEstimate(flops=flops, bytes_accessed=moved, transcendentals=0),
        compiler_params=pltpu.CompilerParams(vmem_limit_bytes=48 << 20),
    )(*arrays)


def array(shape, dtype):
    return jax.ShapeDtypeStruct(shape, dtype)


def swapped(values, axis, distance):
    peers = lax.axis_size(axis)
    return lax.ppermute(values, axis, [(i, i ^ distance) for i in range(peers)])


def pairs_of(peers, first):
    pairs = [(i, i + 1) for i in range(first, peers - 1, 2)]
    return pairs + [(j, i) for i, j in pairs]


def neighbour_rows(fields, width):
    peers = lax.axis_size("row")
    odd = lax.axis_index("row") % 2 == 1
    half = fields.shape[1] // 2
    row_at = lambda at: jnp.concatenate(
        [fields[:, at : at + width], fields[:, half + at : half + at + width]], axis=1
    )
    first, last = row_at(0), row_at(half - width)
    over_odd = lax.ppermute(jnp.where(odd, last, first), "row", pairs_of(peers, 1))
    over_even = lax.ppermute(jnp.where(odd, first, last), "row", pairs_of(peers, 0))
    return jnp.where(odd, over_even, over_odd), jnp.where(odd, over_odd, over_even)


def rounds_of(peers):
    bits = [1 << k for k in reversed(range(peers.bit_length() - 1))]
    head, tail = bits[:-2], bits[-2:]
    last = [tail[0] ^ tail[1], tail[0], tail[1]] if len(tail) == 2 else tail
    return head, last


def gathered_last(values, last):
    return [values] + [swapped(values, "mode", distance) for distance in last]


def pulled_rows(rows, width):
    def fn(taps, own, before, after):
        half = rows * width
        real = [before[:, :width]] + [own[:, j * width : (j + 1) * width] for j in range(rows)]
        imag = [before[:, width:]] + [
            own[:, half + j * width : half + (j + 1) * width] for j in range(rows)
        ]
        real = [part.astype(F32) for part in real + [after[:, :width]]]
        imag = [part.astype(F32) for part in imag + [after[:, width:]]]
        out_real, out_imag = [], []
        for j in range(1, rows + 1):
            sources = (j + 1, j, j - 1)
            total_real = total_imag = 0.0
            for k in range(3):
                a, b = taps[0:1, k : k + 1], taps[1:2, k : k + 1]
                total_real = total_real + a * real[sources[k]] + b * imag[sources[k]]
                total_imag = total_imag + a * imag[sources[k]] - b * real[sources[k]]
            out_real.append(total_real)
            out_imag.append(total_imag)
        return (jnp.concatenate(out_real + out_imag, axis=1).astype(BF16),)

    return fn


def parts_of(pieces, first):
    quarter = pieces[0].shape[1] // 4
    cut = lambda at: [piece[:, at * quarter : (at + 1) * quarter] for piece in pieces]
    return jnp.concatenate(cut(first), axis=0), jnp.concatenate(cut(first + 1), axis=0)


def by_rows(values, width):
    return [values[:, at : at + width] for at in range(0, values.shape[1], width)]


def masked_and_spread(width):
    def fn(cosine, sine, propagator, *pieces):
        real, imag = parts_of(pieces, 0)
        total, half = real.shape
        shape = (total // cosine.shape[0], *cosine.shape)
        real = real.astype(F32).reshape(shape)
        imag = imag.astype(F32).reshape(shape)
        masked_real = (real * cosine - imag * sine).reshape(total, half).astype(BF16)
        masked_imag = (real * sine + imag * cosine).reshape(total, half).astype(BF16)
        masked = jnp.concatenate([masked_real, masked_imag], axis=0)
        stacked = jnp.concatenate(by_rows(masked, width), axis=0)
        over_real = jnp.dot(stacked, propagator[0], preferred_element_type=F32)
        over_imag = jnp.dot(stacked, propagator[1], preferred_element_type=F32)
        out_real, out_imag = [], []
        for at in range(0, stacked.shape[0], 2 * total):
            first, second = slice(at, at + total), slice(at + total, at + 2 * total)
            out_real.append(over_real[first] - over_imag[second])
            out_imag.append(over_imag[first] + over_real[second])
        spread = jnp.concatenate(
            [jnp.concatenate(out_real, axis=1), jnp.concatenate(out_imag, axis=1)], axis=0
        )
        return masked, spread.astype(BF16)

    return fn


def both_parts(stacks):
    cut = lambda stack, part: stack[part * (stack.shape[0] // 2) :][: stack.shape[0] // 2]
    return jnp.concatenate([cut(stack, part) for part in (0, 1) for stack in stacks], axis=0)


def project(width, late):
    def fn(cosine, sine, propagator, early_spread, *pieces):
        masked, spread = masked_and_spread(width)(cosine, sine, propagator, *pieces[-late:])
        spread = both_parts([early_spread, spread])
        targets = jnp.concatenate(parts_of(pieces, 2), axis=0)
        total = targets.shape[0] // 2
        product = lax.dot_general(spread, targets, NT, preferred_element_type=F32)
        real = product[:total, :total] + product[total:, total:]
        imag = product[total:, :total] - product[:total, total:]
        return masked, jnp.concatenate([real, imag], axis=1)

    return fn


def back_propagated(width):
    def fn(propagator, *pieces):
        targets = jnp.concatenate(parts_of(pieces, 2), axis=0)
        total = targets.shape[0] // 2
        stacked = jnp.concatenate(by_rows(targets, width), axis=0)
        over_real = lax.dot_general(stacked, propagator[0], NT, preferred_element_type=F32)
        over_imag = lax.dot_general(stacked, propagator[1], NT, preferred_element_type=F32)
        out_real, out_imag = [], []
        for at in range(0, stacked.shape[0], 2 * total):
            first, second = slice(at, at + total), slice(at + total, at + 2 * total)
            out_real.append(over_real[first] + over_imag[second])
            out_imag.append(over_real[second] - over_imag[first])
        result = jnp.concatenate(
            [jnp.concatenate(out_real, axis=1), jnp.concatenate(out_imag, axis=1)], axis=0
        )
        return (result.astype(BF16),)

    return fn


def finish(local_modes, waves, rows, width, scale_pixels, scale_grad):
    def fn(mask, order, back, early, late, *partials):
        total = mask.shape[0]
        summed = partials[0]
        for part in partials[1:]:
            summed = summed + part
        real = summed[:, :total] * scale_pixels * mask
        imag = summed[:, total:] * scale_pixels * mask
        own = jnp.concatenate([real[:local_modes], imag[:local_modes]], axis=0)
        own = jnp.dot(own, order, precision=lax.Precision.HIGHEST, preferred_element_type=F32)
        coupling = own.reshape(2, local_modes, total)
        weight_real, weight_imag = real.astype(BF16), imag.astype(BF16)
        weights = jnp.concatenate(
            [
                jnp.concatenate([weight_real, -weight_imag], axis=1),
                jnp.concatenate([weight_imag, weight_real], axis=1),
            ],
            axis=0,
        )
        adjoint = jnp.dot(weights, back, preferred_element_type=F32)
        fields = both_parts([early, late]).astype(F32)
        term = fields[total:] * adjoint[:total] - fields[:total] * adjoint[total:]
        group = 2 * waves
        folded = jnp.sum(term.reshape(total // group, group, rows * width), axis=0)
        folded = (folded[:waves] + folded[waves:]) * scale_grad
        grad = jnp.stack(by_rows(folded, width), axis=1)
        return coupling, grad

    return fn


def body(forward, backward, propagator, row_taps, phase_masks, plane_index, wave_ratio, pair_list):
    local_modes, rows, _, width = forward.shape
    waves = wave_ratio.shape[0]
    mode_peers = lax.axis_size("mode")
    row_peers = lax.axis_size("row")
    total = local_modes * mode_peers
    row_total = rows * row_peers
    group_size = total // NG
    half = rows * width

    flat = lambda fields: fields.transpose(0, 2, 1, 3).reshape(fields.shape[0], 2 * half)
    head, last = rounds_of(mode_peers)
    distances = head + last[:2]
    targets, fields = backward, forward
    for distance in head:
        near, far = (targets, fields), [
            swapped(values, "mode", distance) for values in (targets, fields)
        ]
        if targets.ndim > 2:
            near, far = [flat(values) for values in near], [flat(values) for values in far]
        targets, fields = [jnp.concatenate(both, axis=0) for both in zip(near, far)]
    if targets.ndim > 2:
        targets, fields = flat(targets), flat(fields)
    before, after = neighbour_rows(targets, width)
    (pulled,) = local_call(
        pulled_rows(rows, width),
        [array(targets.shape, BF16)],
        [jnp.pad(row_taps, ((0, 6), (0, 125))), targets, before, after],
        flops=24 * targets.shape[0] * half,
    )
    both = jnp.concatenate([fields, pulled], axis=1)
    both, pair_list, plane_index, wave_ratio, phase_masks = lax.optimization_barrier(
        (both, pair_list, plane_index, wave_ratio, phase_masks)
    )
    pieces = gathered_last(both, last)

    planes = jnp.arange(phase_masks.shape[0], dtype=jnp.int32)
    selector = (plane_index[:, None] == planes[None, :]).astype(F32)
    picked = jnp.einsum("wp,prc->wrc", selector, phase_masks, precision=lax.Precision.HIGHEST)
    phases = (picked * wave_ratio[:, None, None]).reshape(waves, half)
    cosine = jnp.tile(jnp.cos(phases), (2, 1))
    sine = jnp.tile(jnp.sin(phases), (2, 1))

    places = jnp.arange(total, dtype=jnp.int32)
    peers = lax.axis_index("mode").astype(jnp.int32)
    for k, distance in enumerate(distances):
        peers = peers ^ ((places // (local_modes << k)) % 2 * distance)
    numbers = peers * local_modes + places % local_modes
    groups = numbers // group_size
    to_target = (pair_list[:, 0][:, None] == groups[None, :]).astype(BF16)
    to_forward = (pair_list[:, 1][:, None] == groups[None, :]).astype(BF16)
    mask = lax.dot_general(
        to_forward, to_target, (((0,), (0,)), ((), ())), preferred_element_type=F32
    )
    order = (numbers[:, None] == places[None, :]).astype(F32)

    early = (len(pieces) + 1) // 2
    late = len(pieces) - early
    early_total, late_total = early * both.shape[0], late * both.shape[0]
    early_masked, early_spread = local_call(
        masked_and_spread(width),
        [array((2 * early_total, half), BF16)] * 2,
        [cosine, sine, propagator, *pieces[:early]],
        flops=8 * early_total * half * width,
    )
    late_masked, partial = local_call(
        project(width, late),
        [array((2 * late_total, half), BF16), array((total, 2 * total), F32)],
        [cosine, sine, propagator, early_spread, *pieces],
        flops=8 * late_total * half * width + 8 * total * total * half,
    )
    partials = [partial] + [swapped(partial, "row", d) for d in range(row_peers - 1, 0, -1)]
    (back,) = local_call(
        back_propagated(width),
        [array((2 * total, half), BF16)],
        [propagator, *pieces],
        flops=8 * total * half * width,
    )
    coupling, mask_grad = local_call(
        finish(
            local_modes,
            waves,
            rows,
            width,
            1.0 / math.sqrt(row_total * width),
            -2.0 / total,
        ),
        [array((2, local_modes, total), F32), array((waves, rows, width), F32)],
        [mask, order, back, early_masked, late_masked, *partials],
        flops=8 * total * total * half,
    )
    return coupling, mask_grad


def solution(mesh):
    in_specs = (
        P("mode", "row", None, None),
        P("mode", "row", None, None),
        P(),
        P(),
        P(None, "row", None),
        P(),
        P(),
        P(),
    )
    out_specs = (P(None, "mode", None), P(None, "row", None))
    return jax.shard_map(body, mesh=mesh, in_specs=in_specs, out_specs=out_specs, check_vma=False)
```

```python
import math

import jax
import jax.numpy as jnp
from jax import lax
from jax.experimental import pallas as pl
from jax.experimental.pallas import tpu as pltpu
from jax.sharding import PartitionSpec as P

NG = 16
VMEM_BYTES = 24 << 20
NT = (((1,), (1,)), ((), ()))
F32 = jnp.float32
BF16 = jnp.bfloat16


def size_of(item):
    return math.prod(item.shape) * jnp.dtype(item.dtype).itemsize


def local_call(fn, outs, arrays, flops=0):
    moved = sum(size_of(item) for item in (*arrays, *outs))
    if moved > VMEM_BYTES:
        return fn(*arrays)
    count = len(arrays)

    def kernel(*refs):
        values = fn(*[ref[...] for ref in refs[:count]])
        for ref, value in zip(refs[count:], values):
            ref[...] = value

    return pl.pallas_call(
        kernel,
        out_shape=tuple(outs),
        in_specs=[pl.BlockSpec(memory_space=pltpu.VMEM)] * count,
        out_specs=tuple(pl.BlockSpec(memory_space=pltpu.VMEM) for _ in outs),
        cost_estimate=pl.CostEstimate(flops=flops, bytes_accessed=moved, transcendentals=0),
        compiler_params=pltpu.CompilerParams(vmem_limit_bytes=48 << 20),
    )(*arrays)


def array(shape, dtype):
    return jax.ShapeDtypeStruct(shape, dtype)


def swapped(values, axis, distance):
    peers = lax.axis_size(axis)
    return lax.ppermute(values, axis, [(i, i ^ distance) for i in range(peers)])


def pairs_of(peers, first):
    pairs = [(i, i + 1) for i in range(first, peers - 1, 2)]
    return pairs + [(j, i) for i, j in pairs]


def neighbour_rows(fields, width):
    peers = lax.axis_size("row")
    odd = lax.axis_index("row") % 2 == 1
    half = fields.shape[1] // 2
    row_at = lambda at: jnp.concatenate(
        [fields[:, at : at + width], fields[:, half + at : half + at + width]], axis=1
    )
    first, last = row_at(0), row_at(half - width)
    over_odd = lax.ppermute(jnp.where(odd, last, first), "row", pairs_of(peers, 1))
    over_even = lax.ppermute(jnp.where(odd, first, last), "row", pairs_of(peers, 0))
    return jnp.where(odd, over_even, over_odd), jnp.where(odd, over_odd, over_even)


def rounds_of(peers):
    bits = [1 << k for k in reversed(range(peers.bit_length() - 1))]
    head, tail = bits[:-2], bits[-2:]
    last = [tail[0] ^ tail[1], tail[0], tail[1]] if len(tail) == 2 else tail
    return head, last


def gathered_last(values, last):
    return [values] + [swapped(values, "mode", distance) for distance in last]


def pulled_rows(rows, width):
    def fn(taps, own, before, after):
        half = rows * width
        real = [before[:, :width]] + [own[:, j * width : (j + 1) * width] for j in range(rows)]
        imag = [before[:, width:]] + [
            own[:, half + j * width : half + (j + 1) * width] for j in range(rows)
        ]
        real = [part.astype(F32) for part in real + [after[:, :width]]]
        imag = [part.astype(F32) for part in imag + [after[:, width:]]]
        out_real, out_imag = [], []
        for j in range(1, rows + 1):
            sources = (j + 1, j, j - 1)
            total_real = total_imag = 0.0
            for k in range(3):
                a, b = taps[0:1, k : k + 1], taps[1:2, k : k + 1]
                total_real = total_real + a * real[sources[k]] + b * imag[sources[k]]
                total_imag = total_imag + a * imag[sources[k]] - b * real[sources[k]]
            out_real.append(total_real)
            out_imag.append(total_imag)
        return (jnp.concatenate(out_real + out_imag, axis=1).astype(BF16),)

    return fn


def parts_of(pieces, first):
    quarter = pieces[0].shape[1] // 4
    cut = lambda at: [piece[:, at * quarter : (at + 1) * quarter] for piece in pieces]
    return jnp.concatenate(cut(first), axis=0), jnp.concatenate(cut(first + 1), axis=0)


def by_rows(values, width):
    return [values[:, at : at + width] for at in range(0, values.shape[1], width)]


def masked_and_spread(width):
    def fn(cosine, sine, propagator, *pieces):
        real, imag = parts_of(pieces, 0)
        total, half = real.shape
        shape = (total // cosine.shape[0], *cosine.shape)
        real = real.astype(F32).reshape(shape)
        imag = imag.astype(F32).reshape(shape)
        masked_real = (real * cosine - imag * sine).reshape(total, half).astype(BF16)
        masked_imag = (real * sine + imag * cosine).reshape(total, half).astype(BF16)
        masked = jnp.concatenate([masked_real, masked_imag], axis=0)
        stacked = jnp.concatenate(by_rows(masked, width), axis=0)
        over_real = jnp.dot(stacked, propagator[0], preferred_element_type=F32)
        over_imag = jnp.dot(stacked, propagator[1], preferred_element_type=F32)
        out_real, out_imag = [], []
        for at in range(0, stacked.shape[0], 2 * total):
            first, second = slice(at, at + total), slice(at + total, at + 2 * total)
            out_real.append(over_real[first] - over_imag[second])
            out_imag.append(over_imag[first] + over_real[second])
        spread = jnp.concatenate(
            [jnp.concatenate(out_real, axis=1), jnp.concatenate(out_imag, axis=1)], axis=0
        )
        return masked, spread.astype(BF16)

    return fn


def both_parts(stacks):
    cut = lambda stack, part: stack[part * (stack.shape[0] // 2) :][: stack.shape[0] // 2]
    return jnp.concatenate([cut(stack, part) for part in (0, 1) for stack in stacks], axis=0)


def project(width, late):
    def fn(cosine, sine, propagator, early_spread, *pieces):
        masked, spread = masked_and_spread(width)(cosine, sine, propagator, *pieces[-late:])
        spread = both_parts([early_spread, spread])
        targets = jnp.concatenate(parts_of(pieces, 2), axis=0)
        total = targets.shape[0] // 2
        product = lax.dot_general(spread, targets, NT, preferred_element_type=F32)
        real = product[:total, :total] + product[total:, total:]
        imag = product[total:, :total] - product[:total, total:]
        return masked, jnp.concatenate([real, imag], axis=1)

    return fn


def back_propagated(width):
    def fn(propagator, *pieces):
        targets = jnp.concatenate(parts_of(pieces, 2), axis=0)
        total = targets.shape[0] // 2
        stacked = jnp.concatenate(by_rows(targets, width), axis=0)
        over_real = lax.dot_general(stacked, propagator[0], NT, preferred_element_type=F32)
        over_imag = lax.dot_general(stacked, propagator[1], NT, preferred_element_type=F32)
        out_real, out_imag = [], []
        for at in range(0, stacked.shape[0], 2 * total):
            first, second = slice(at, at + total), slice(at + total, at + 2 * total)
            out_real.append(over_real[first] + over_imag[second])
            out_imag.append(over_real[second] - over_imag[first])
        result = jnp.concatenate(
            [jnp.concatenate(out_real, axis=1), jnp.concatenate(out_imag, axis=1)], axis=0
        )
        return (result.astype(BF16),)

    return fn


def finish(local_modes, waves, rows, width, scale_pixels, scale_grad):
    def fn(mask, order, back, early, late, *partials):
        total = mask.shape[0]
        summed = partials[0]
        for part in partials[1:]:
            summed = summed + part
        real = summed[:, :total] * scale_pixels * mask
        imag = summed[:, total:] * scale_pixels * mask
        own = jnp.concatenate([real[:local_modes], imag[:local_modes]], axis=0)
        high = own.astype(BF16)
        rest = own - high.astype(F32)
        middle = rest.astype(BF16)
        low = (rest - middle.astype(F32)).astype(BF16)
        sorted_parts = jnp.dot(
            jnp.concatenate([high, middle, low], axis=0), order, preferred_element_type=F32
        )
        size = own.shape[0]
        own = sorted_parts[:size] + sorted_parts[size : 2 * size] + sorted_parts[2 * size :]
        coupling = own.reshape(2, local_modes, total)
        weight_real, weight_imag = real.astype(BF16), imag.astype(BF16)
        weights = jnp.concatenate(
            [
                jnp.concatenate([weight_real, -weight_imag], axis=1),
                jnp.concatenate([weight_imag, weight_real], axis=1),
            ],
            axis=0,
        )
        adjoint = jnp.dot(weights, back, preferred_element_type=F32)
        fields = both_parts([early, late]).astype(F32)
        term = fields[total:] * adjoint[:total] - fields[:total] * adjoint[total:]
        group = 2 * waves
        folded = jnp.sum(term.reshape(total // group, group, rows * width), axis=0)
        folded = (folded[:waves] + folded[waves:]) * scale_grad
        grad = jnp.stack(by_rows(folded, width), axis=1)
        return coupling, grad

    return fn


def body(forward, backward, propagator, row_taps, phase_masks, plane_index, wave_ratio, pair_list):
    local_modes, rows, _, width = forward.shape
    waves = wave_ratio.shape[0]
    mode_peers = lax.axis_size("mode")
    row_peers = lax.axis_size("row")
    total = local_modes * mode_peers
    row_total = rows * row_peers
    group_size = total // NG
    half = rows * width

    flat = lambda fields: fields.transpose(0, 2, 1, 3).reshape(fields.shape[0], 2 * half)
    head, last = rounds_of(mode_peers)
    distances = head + last[:2]
    targets, fields = backward, forward
    for distance in head:
        near, far = (targets, fields), [
            swapped(values, "mode", distance) for values in (targets, fields)
        ]
        if targets.ndim > 2:
            near, far = [flat(values) for values in near], [flat(values) for values in far]
        targets, fields = [jnp.concatenate(both, axis=0) for both in zip(near, far)]
    if targets.ndim > 2:
        targets, fields = flat(targets), flat(fields)
    before, after = neighbour_rows(targets, width)
    (pulled,) = local_call(
        pulled_rows(rows, width),
        [array(targets.shape, BF16)],
        [jnp.pad(row_taps, ((0, 6), (0, 125))), targets, before, after],
        flops=24 * targets.shape[0] * half,
    )
    both = jnp.concatenate([fields, pulled], axis=1)
    both, pair_list, plane_index, wave_ratio, phase_masks = lax.optimization_barrier(
        (both, pair_list, plane_index, wave_ratio, phase_masks)
    )
    pieces = gathered_last(both, last)

    planes = jnp.arange(phase_masks.shape[0], dtype=jnp.int32)
    selector = (plane_index[:, None] == planes[None, :]).astype(F32)
    picked = jnp.einsum("wp,prc->wrc", selector, phase_masks, precision=lax.Precision.HIGHEST)
    phases = (picked * wave_ratio[:, None, None]).reshape(waves, half)
    cosine = jnp.tile(jnp.cos(phases), (2, 1))
    sine = jnp.tile(jnp.sin(phases), (2, 1))

    places = jnp.arange(total, dtype=jnp.int32)
    peers = lax.axis_index("mode").astype(jnp.int32)
    for k, distance in enumerate(distances):
        peers = peers ^ ((places // (local_modes << k)) % 2 * distance)
    numbers = peers * local_modes + places % local_modes
    groups = numbers // group_size
    to_target = (pair_list[:, 0][:, None] == groups[None, :]).astype(BF16)
    to_forward = (pair_list[:, 1][:, None] == groups[None, :]).astype(BF16)
    mask = lax.dot_general(
        to_forward, to_target, (((0,), (0,)), ((), ())), preferred_element_type=F32
    )
    order = (numbers[:, None] == places[None, :]).astype(BF16)

    early = (len(pieces) + 1) // 2
    late = len(pieces) - early
    early_total, late_total = early * both.shape[0], late * both.shape[0]
    early_masked, early_spread = local_call(
        masked_and_spread(width),
        [array((2 * early_total, half), BF16)] * 2,
        [cosine, sine, propagator, *pieces[:early]],
        flops=8 * early_total * half * width,
    )
    late_masked, partial = local_call(
        project(width, late),
        [array((2 * late_total, half), BF16), array((total, 2 * total), F32)],
        [cosine, sine, propagator, early_spread, *pieces],
        flops=8 * late_total * half * width + 8 * total * total * half,
    )
    partials = [partial] + [swapped(partial, "row", d) for d in range(row_peers - 1, 0, -1)]
    (back,) = local_call(
        back_propagated(width),
        [array((2 * total, half), BF16)],
        [propagator, *pieces],
        flops=8 * total * half * width,
    )
    coupling, mask_grad = local_call(
        finish(
            local_modes,
            waves,
            rows,
            width,
            1.0 / math.sqrt(row_total * width),
            -2.0 / total,
        ),
        [array((2, local_modes, total), F32), array((waves, rows, width), F32)],
        [mask, order, back, early_masked, late_masked, *partials],
        flops=8 * total * total * half,
    )
    return coupling, mask_grad


def solution(mesh):
    in_specs = (
        P("mode", "row", None, None),
        P("mode", "row", None, None),
        P(),
        P(),
        P(None, "row", None),
        P(),
        P(),
        P(),
    )
    out_specs = (P(None, "mode", None), P(None, "row", None))
    return jax.shard_map(body, mesh=mesh, in_specs=in_specs, out_specs=out_specs, check_vma=False)
```

```python
import math

import jax
import jax.numpy as jnp
from jax import lax
from jax.experimental import pallas as pl
from jax.experimental.pallas import tpu as pltpu
from jax.sharding import PartitionSpec as P

NG = 16
VMEM_BYTES = 24 << 20
NT = (((1,), (1,)), ((), ()))
F32 = jnp.float32
BF16 = jnp.bfloat16


def size_of(item):
    return math.prod(item.shape) * jnp.dtype(item.dtype).itemsize


def local_call(fn, outs, arrays, flops=0):
    moved = sum(size_of(item) for item in (*arrays, *outs))
    if moved > VMEM_BYTES:
        return fn(*arrays)
    count = len(arrays)

    def kernel(*refs):
        values = fn(*[ref[...] for ref in refs[:count]])
        for ref, value in zip(refs[count:], values):
            ref[...] = value

    return pl.pallas_call(
        kernel,
        out_shape=tuple(outs),
        in_specs=[pl.BlockSpec(memory_space=pltpu.VMEM)] * count,
        out_specs=tuple(pl.BlockSpec(memory_space=pltpu.VMEM) for _ in outs),
        cost_estimate=pl.CostEstimate(flops=flops, bytes_accessed=moved, transcendentals=0),
        compiler_params=pltpu.CompilerParams(vmem_limit_bytes=48 << 20),
    )(*arrays)


def array(shape, dtype):
    return jax.ShapeDtypeStruct(shape, dtype)


def swapped(values, axis, distance):
    peers = lax.axis_size(axis)
    return lax.ppermute(values, axis, [(i, i ^ distance) for i in range(peers)])


def pairs_of(peers, first):
    pairs = [(i, i + 1) for i in range(first, peers - 1, 2)]
    return pairs + [(j, i) for i, j in pairs]


def neighbour_rows(fields, width):
    peers = lax.axis_size("row")
    odd = lax.axis_index("row") % 2 == 1
    half = fields.shape[1] // 2
    row_at = lambda at: jnp.concatenate(
        [fields[:, at : at + width], fields[:, half + at : half + at + width]], axis=1
    )
    first, last = row_at(0), row_at(half - width)
    over_odd = lax.ppermute(jnp.where(odd, last, first), "row", pairs_of(peers, 1))
    over_even = lax.ppermute(jnp.where(odd, first, last), "row", pairs_of(peers, 0))
    return over_even, over_odd


def rounds_of(peers):
    bits = [1 << k for k in reversed(range(peers.bit_length() - 1))]
    head, tail = bits[:-2], bits[-2:]
    last = [tail[0] ^ tail[1], tail[0], tail[1]] if len(tail) == 2 else tail
    return head, last


def gathered_last(values, last):
    return [values] + [swapped(values, "mode", distance) for distance in last]


def pulled_rows(rows, width):
    def fn(taps, fields, own, over_even, over_odd):
        half = rows * width
        odd = jnp.broadcast_to(taps[2:3, 0:1], over_even.shape) > 0.5
        before = jnp.where(odd, over_even.astype(F32), over_odd.astype(F32))
        after = jnp.where(odd, over_odd.astype(F32), over_even.astype(F32))
        real = [before[:, :width]] + [own[:, j * width : (j + 1) * width] for j in range(rows)]
        imag = [before[:, width:]] + [
            own[:, half + j * width : half + (j + 1) * width] for j in range(rows)
        ]
        real = [part.astype(F32) for part in real + [after[:, :width]]]
        imag = [part.astype(F32) for part in imag + [after[:, width:]]]
        out_real, out_imag = [], []
        for j in range(1, rows + 1):
            sources = (j + 1, j, j - 1)
            total_real = total_imag = 0.0
            for k in range(3):
                a, b = taps[0:1, k : k + 1], taps[1:2, k : k + 1]
                total_real = total_real + a * real[sources[k]] + b * imag[sources[k]]
                total_imag = total_imag + a * imag[sources[k]] - b * real[sources[k]]
            out_real.append(total_real)
            out_imag.append(total_imag)
        pulled = jnp.concatenate(out_real + out_imag, axis=1).astype(BF16)
        return (jnp.concatenate([fields, pulled], axis=1),)

    return fn


def parts_of(pieces, first):
    quarter = pieces[0].shape[1] // 4
    cut = lambda at: [piece[:, at * quarter : (at + 1) * quarter] for piece in pieces]
    return jnp.concatenate(cut(first), axis=0), jnp.concatenate(cut(first + 1), axis=0)


def by_rows(values, width):
    return [values[:, at : at + width] for at in range(0, values.shape[1], width)]


def masked_and_spread(width):
    def fn(cosine, sine, propagator, *pieces):
        real, imag = parts_of(pieces, 0)
        total, half = real.shape
        shape = (total // cosine.shape[0], *cosine.shape)
        real = real.astype(F32).reshape(shape)
        imag = imag.astype(F32).reshape(shape)
        masked_real = (real * cosine - imag * sine).reshape(total, half).astype(BF16)
        masked_imag = (real * sine + imag * cosine).reshape(total, half).astype(BF16)
        masked = jnp.concatenate([masked_real, masked_imag], axis=0)
        stacked = jnp.concatenate(by_rows(masked, width), axis=0)
        over_real = jnp.dot(stacked, propagator[0], preferred_element_type=F32)
        over_imag = jnp.dot(stacked, propagator[1], preferred_element_type=F32)
        out_real, out_imag = [], []
        for at in range(0, stacked.shape[0], 2 * total):
            first, second = slice(at, at + total), slice(at + total, at + 2 * total)
            out_real.append(over_real[first] - over_imag[second])
            out_imag.append(over_imag[first] + over_real[second])
        spread = jnp.concatenate(
            [jnp.concatenate(out_real, axis=1), jnp.concatenate(out_imag, axis=1)], axis=0
        )
        return masked, spread.astype(BF16)

    return fn


def both_parts(stacks):
    cut = lambda stack, part: stack[part * (stack.shape[0] // 2) :][: stack.shape[0] // 2]
    return jnp.concatenate([cut(stack, part) for part in (0, 1) for stack in stacks], axis=0)


def project(width, late):
    def fn(cosine, sine, propagator, early_spread, *pieces):
        masked, spread = masked_and_spread(width)(cosine, sine, propagator, *pieces[-late:])
        spread = both_parts([early_spread, spread])
        targets = jnp.concatenate(parts_of(pieces, 2), axis=0)
        total = targets.shape[0] // 2
        product = lax.dot_general(spread, targets, NT, preferred_element_type=F32)
        real = product[:total, :total] + product[total:, total:]
        imag = product[total:, :total] - product[:total, total:]
        return masked, jnp.concatenate([real, imag], axis=1)

    return fn


def back_propagated(width):
    def fn(propagator, *pieces):
        targets = jnp.concatenate(parts_of(pieces, 2), axis=0)
        total = targets.shape[0] // 2
        stacked = jnp.concatenate(by_rows(targets, width), axis=0)
        over_real = lax.dot_general(stacked, propagator[0], NT, preferred_element_type=F32)
        over_imag = lax.dot_general(stacked, propagator[1], NT, preferred_element_type=F32)
        out_real, out_imag = [], []
        for at in range(0, stacked.shape[0], 2 * total):
            first, second = slice(at, at + total), slice(at + total, at + 2 * total)
            out_real.append(over_real[first] + over_imag[second])
            out_imag.append(over_real[second] - over_imag[first])
        result = jnp.concatenate(
            [jnp.concatenate(out_real, axis=1), jnp.concatenate(out_imag, axis=1)], axis=0
        )
        return (result.astype(BF16),)

    return fn


def finish(local_modes, waves, rows, width, scale_pixels, scale_grad):
    def fn(mask, order, back, early, late, *partials):
        total = mask.shape[0]
        summed = partials[0]
        for part in partials[1:]:
            summed = summed + part
        real = summed[:, :total] * scale_pixels * mask
        imag = summed[:, total:] * scale_pixels * mask
        own = jnp.concatenate([real[:local_modes], imag[:local_modes]], axis=0)
        high = own.astype(BF16)
        rest = own - high.astype(F32)
        middle = rest.astype(BF16)
        low = (rest - middle.astype(F32)).astype(BF16)
        sorted_parts = jnp.dot(
            jnp.concatenate([high, middle, low], axis=0), order, preferred_element_type=F32
        )
        size = own.shape[0]
        own = sorted_parts[:size] + sorted_parts[size : 2 * size] + sorted_parts[2 * size :]
        coupling = own.reshape(2, local_modes, total)
        weight_real, weight_imag = real.astype(BF16), imag.astype(BF16)
        weights = jnp.concatenate(
            [
                jnp.concatenate([weight_real, -weight_imag], axis=1),
                jnp.concatenate([weight_imag, weight_real], axis=1),
            ],
            axis=0,
        )
        adjoint = jnp.dot(weights, back, preferred_element_type=F32)
        fields = both_parts([early, late]).astype(F32)
        term = fields[total:] * adjoint[:total] - fields[:total] * adjoint[total:]
        group = 2 * waves
        folded = jnp.sum(term.reshape(total // group, group, rows * width), axis=0)
        folded = (folded[:waves] + folded[waves:]) * scale_grad
        grad = jnp.stack(by_rows(folded, width), axis=1)
        return coupling, grad

    return fn


def body(forward, backward, propagator, row_taps, phase_masks, plane_index, wave_ratio, pair_list):
    local_modes, rows, _, width = forward.shape
    waves = wave_ratio.shape[0]
    mode_peers = lax.axis_size("mode")
    row_peers = lax.axis_size("row")
    total = local_modes * mode_peers
    row_total = rows * row_peers
    group_size = total // NG
    half = rows * width

    flat = lambda fields: fields.transpose(0, 2, 1, 3).reshape(fields.shape[0], 2 * half)
    head, last = rounds_of(mode_peers)
    distances = head + last[:2]
    targets, fields = backward, forward
    for distance in head:
        near, far = (targets, fields), [
            swapped(values, "mode", distance) for values in (targets, fields)
        ]
        if targets.ndim > 2:
            near, far = [flat(values) for values in near], [flat(values) for values in far]
        targets, fields = [jnp.concatenate(both, axis=0) for both in zip(near, far)]
    if targets.ndim > 2:
        targets, fields = flat(targets), flat(fields)
    over_even, over_odd = neighbour_rows(targets, width)
    odd = (lax.axis_index("row") % 2).astype(F32)
    taps = jnp.concatenate([row_taps, jnp.full((1, row_taps.shape[1]), odd)], axis=0)
    (both,) = local_call(
        pulled_rows(rows, width),
        [array((targets.shape[0], 4 * half), BF16)],
        [jnp.pad(taps, ((0, 5), (0, 125))), fields, targets, over_even, over_odd],
        flops=24 * targets.shape[0] * half,
    )
    both, pair_list, plane_index, wave_ratio, phase_masks = lax.optimization_barrier(
        (both, pair_list, plane_index, wave_ratio, phase_masks)
    )
    pieces = gathered_last(both, last)

    planes = jnp.arange(phase_masks.shape[0], dtype=jnp.int32)
    selector = (plane_index[:, None] == planes[None, :]).astype(F32)
    picked = jnp.einsum("wp,prc->wrc", selector, phase_masks, precision=lax.Precision.HIGHEST)
    phases = (picked * wave_ratio[:, None, None]).reshape(waves, half)
    cosine = jnp.tile(jnp.cos(phases), (2, 1))
    sine = jnp.tile(jnp.sin(phases), (2, 1))

    places = jnp.arange(total, dtype=jnp.int32)
    peers = lax.axis_index("mode").astype(jnp.int32)
    for k, distance in enumerate(distances):
        peers = peers ^ ((places // (local_modes << k)) % 2 * distance)
    numbers = peers * local_modes + places % local_modes
    groups = numbers // group_size
    to_target = (pair_list[:, 0][:, None] == groups[None, :]).astype(BF16)
    to_forward = (pair_list[:, 1][:, None] == groups[None, :]).astype(BF16)
    mask = lax.dot_general(
        to_forward, to_target, (((0,), (0,)), ((), ())), preferred_element_type=F32
    )
    order = (numbers[:, None] == places[None, :]).astype(BF16)

    early = len(pieces) - 1
    late = len(pieces) - early
    early_total, late_total = early * both.shape[0], late * both.shape[0]
    early_masked, early_spread = local_call(
        masked_and_spread(width),
        [array((2 * early_total, half), BF16)] * 2,
        [cosine, sine, propagator, *pieces[:early]],
        flops=8 * early_total * half * width,
    )
    late_masked, partial = local_call(
        project(width, late),
        [array((2 * late_total, half), BF16), array((total, 2 * total), F32)],
        [cosine, sine, propagator, early_spread, *pieces],
        flops=8 * late_total * half * width + 8 * total * total * half,
    )
    partials = [partial] + [swapped(partial, "row", d) for d in range(row_peers - 1, 0, -1)]
    (back,) = local_call(
        back_propagated(width),
        [array((2 * total, half), BF16)],
        [propagator, *pieces],
        flops=8 * total * half * width,
    )
    coupling, mask_grad = local_call(
        finish(
            local_modes,
            waves,
            rows,
            width,
            1.0 / math.sqrt(row_total * width),
            -2.0 / total,
        ),
        [array((2, local_modes, total), F32), array((waves, rows, width), F32)],
        [mask, order, back, early_masked, late_masked, *partials],
        flops=8 * total * total * half,
    )
    return coupling, mask_grad


def solution(mesh):
    in_specs = (
        P("mode", "row", None, None),
        P("mode", "row", None, None),
        P(),
        P(),
        P(None, "row", None),
        P(),
        P(),
        P(),
    )
    out_specs = (P(None, "mode", None), P(None, "row", None))
    return jax.shard_map(body, mesh=mesh, in_specs=in_specs, out_specs=out_specs, check_vma=False)
```

```python
import math

import jax
import jax.numpy as jnp
from jax import lax
from jax.experimental import pallas as pl
from jax.experimental.pallas import tpu as pltpu
from jax.sharding import PartitionSpec as P

NG = 16
VMEM_BYTES = 24 << 20
NT = (((1,), (1,)), ((), ()))
F32 = jnp.float32
BF16 = jnp.bfloat16


def size_of(item):
    return math.prod(item.shape) * jnp.dtype(item.dtype).itemsize


def local_call(fn, outs, arrays, flops=0):
    moved = sum(size_of(item) for item in (*arrays, *outs))
    if moved > VMEM_BYTES:
        return fn(*arrays)
    count = len(arrays)

    def kernel(*refs):
        values = fn(*[ref[...] for ref in refs[:count]])
        for ref, value in zip(refs[count:], values):
            ref[...] = value

    return pl.pallas_call(
        kernel,
        out_shape=tuple(outs),
        in_specs=[pl.BlockSpec(memory_space=pltpu.VMEM)] * count,
        out_specs=tuple(pl.BlockSpec(memory_space=pltpu.VMEM) for _ in outs),
        cost_estimate=pl.CostEstimate(flops=flops, bytes_accessed=moved, transcendentals=0),
        compiler_params=pltpu.CompilerParams(vmem_limit_bytes=48 << 20),
    )(*arrays)


def array(shape, dtype):
    return jax.ShapeDtypeStruct(shape, dtype)


def swapped(values, axis, distance):
    peers = lax.axis_size(axis)
    return lax.ppermute(values, axis, [(i, i ^ distance) for i in range(peers)])


def pairs_of(peers, first):
    pairs = [(i, i + 1) for i in range(first, peers - 1, 2)]
    return pairs + [(j, i) for i, j in pairs]


def neighbour_rows(fields, width):
    peers = lax.axis_size("row")
    odd = lax.axis_index("row") % 2 == 1
    half = fields.shape[1] // 2
    row_at = lambda at: jnp.concatenate(
        [fields[:, at : at + width], fields[:, half + at : half + at + width]], axis=1
    )
    first, last = row_at(0), row_at(half - width)
    over_odd = lax.ppermute(jnp.where(odd, last, first), "row", pairs_of(peers, 1))
    over_even = lax.ppermute(jnp.where(odd, first, last), "row", pairs_of(peers, 0))
    return over_even, over_odd


def rounds_of(peers):
    bits = [1 << k for k in reversed(range(peers.bit_length() - 1))]
    head, tail = bits[:-2], bits[-2:]
    last = [tail[0] ^ tail[1], tail[0], tail[1]] if len(tail) == 2 else tail
    return head, last


def gathered_last(values, last):
    return [values] + [swapped(values, "mode", distance) for distance in last]


def pulled_rows(rows, width):
    def fn(taps, fields, own, over_even, over_odd):
        half = rows * width
        odd = jnp.broadcast_to(taps[2:3, 0:1], over_even.shape) > 0.5
        before = jnp.where(odd, over_even.astype(F32), over_odd.astype(F32))
        after = jnp.where(odd, over_odd.astype(F32), over_even.astype(F32))
        real = [before[:, :width]] + [own[:, j * width : (j + 1) * width] for j in range(rows)]
        imag = [before[:, width:]] + [
            own[:, half + j * width : half + (j + 1) * width] for j in range(rows)
        ]
        real = [part.astype(F32) for part in real + [after[:, :width]]]
        imag = [part.astype(F32) for part in imag + [after[:, width:]]]
        out_real, out_imag = [], []
        for j in range(1, rows + 1):
            sources = (j + 1, j, j - 1)
            total_real = total_imag = 0.0
            for k in range(3):
                a, b = taps[0:1, k : k + 1], taps[1:2, k : k + 1]
                total_real = total_real + a * real[sources[k]] + b * imag[sources[k]]
                total_imag = total_imag + a * imag[sources[k]] - b * real[sources[k]]
            out_real.append(total_real)
            out_imag.append(total_imag)
        pulled = jnp.concatenate(out_real + out_imag, axis=1).astype(BF16)
        return (jnp.concatenate([fields, pulled], axis=1),)

    return fn


def parts_of(pieces, first):
    quarter = pieces[0].shape[1] // 4
    cut = lambda at: [piece[:, at * quarter : (at + 1) * quarter] for piece in pieces]
    return jnp.concatenate(cut(first), axis=0), jnp.concatenate(cut(first + 1), axis=0)


def by_rows(values, width):
    return [values[:, at : at + width] for at in range(0, values.shape[1], width)]


def masked_and_spread(width):
    def fn(cosine, sine, propagator, *pieces):
        real, imag = parts_of(pieces, 0)
        total, half = real.shape
        shape = (total // cosine.shape[0], *cosine.shape)
        real = real.astype(F32).reshape(shape)
        imag = imag.astype(F32).reshape(shape)
        masked_real = (real * cosine - imag * sine).reshape(total, half).astype(BF16)
        masked_imag = (real * sine + imag * cosine).reshape(total, half).astype(BF16)
        masked = jnp.concatenate([masked_real, masked_imag], axis=0)
        stacked = jnp.concatenate(by_rows(masked, width), axis=0)
        over_real = jnp.dot(stacked, propagator[0], preferred_element_type=F32)
        over_imag = jnp.dot(stacked, propagator[1], preferred_element_type=F32)
        out_real, out_imag = [], []
        for at in range(0, stacked.shape[0], 2 * total):
            first, second = slice(at, at + total), slice(at + total, at + 2 * total)
            out_real.append(over_real[first] - over_imag[second])
            out_imag.append(over_imag[first] + over_real[second])
        spread = jnp.concatenate(
            [jnp.concatenate(out_real, axis=1), jnp.concatenate(out_imag, axis=1)], axis=0
        )
        return masked, spread.astype(BF16)

    return fn


def both_parts(stacks):
    cut = lambda stack, part: stack[part * (stack.shape[0] // 2) :][: stack.shape[0] // 2]
    return jnp.concatenate([cut(stack, part) for part in (0, 1) for stack in stacks], axis=0)


def project(width, late):
    def fn(cosine, sine, propagator, early_spread, *pieces):
        masked, spread = masked_and_spread(width)(cosine, sine, propagator, *pieces[-late:])
        spread = both_parts([early_spread, spread])
        targets = jnp.concatenate(parts_of(pieces, 2), axis=0)
        total = targets.shape[0] // 2
        product = lax.dot_general(spread, targets, NT, preferred_element_type=F32)
        real = product[:total, :total] + product[total:, total:]
        imag = product[total:, :total] - product[:total, total:]
        return masked, jnp.concatenate([real, imag], axis=1)

    return fn


def back_propagated(width):
    def fn(propagator, *pieces):
        targets = jnp.concatenate(parts_of(pieces, 2), axis=0)
        total = targets.shape[0] // 2
        stacked = jnp.concatenate(by_rows(targets, width), axis=0)
        over_real = lax.dot_general(stacked, propagator[0], NT, preferred_element_type=F32)
        over_imag = lax.dot_general(stacked, propagator[1], NT, preferred_element_type=F32)
        out_real, out_imag = [], []
        for at in range(0, stacked.shape[0], 2 * total):
            first, second = slice(at, at + total), slice(at + total, at + 2 * total)
            out_real.append(over_real[first] + over_imag[second])
            out_imag.append(over_real[second] - over_imag[first])
        result = jnp.concatenate(
            [jnp.concatenate(out_real, axis=1), jnp.concatenate(out_imag, axis=1)], axis=0
        )
        return (result.astype(BF16),)

    return fn


def couple(local_modes, scale_pixels, exact_parts):
    def fn(mask, order, *partials):
        total = mask.shape[0]
        summed = partials[0]
        for part in partials[1:]:
            summed = summed + part
        real = summed[:, :total] * scale_pixels * mask
        imag = summed[:, total:] * scale_pixels * mask
        own = jnp.concatenate([real[:local_modes], imag[:local_modes]], axis=0)
        if exact_parts:
            high = own.astype(BF16)
            rest = own - high.astype(F32)
            middle = rest.astype(BF16)
            low = (rest - middle.astype(F32)).astype(BF16)
            parts = jnp.concatenate([high, middle, low], axis=0)
            parts = jnp.dot(parts, order, preferred_element_type=F32)
            size = own.shape[0]
            own = parts[:size] + parts[size : 2 * size] + parts[2 * size :]
        else:
            own = jnp.dot(own, order.astype(F32), precision=lax.Precision.HIGHEST)
        weight_real, weight_imag = real.astype(BF16), imag.astype(BF16)
        weights = jnp.concatenate(
            [
                jnp.concatenate([weight_real, -weight_imag], axis=1),
                jnp.concatenate([weight_imag, weight_real], axis=1),
            ],
            axis=0,
        )
        return own.reshape(2, local_modes, total), weights

    return fn


def gradient(waves, rows, width, scale_grad):
    def fn(weights, back, early, late):
        total = weights.shape[0] // 2
        adjoint = jnp.dot(weights, back, preferred_element_type=F32)
        fields = both_parts([early, late]).astype(F32)
        term = fields[total:] * adjoint[:total] - fields[:total] * adjoint[total:]
        group = 2 * waves
        folded = jnp.sum(term.reshape(total // group, group, rows * width), axis=0)
        folded = (folded[:waves] + folded[waves:]) * scale_grad
        return jnp.stack(by_rows(folded, width), axis=1)

    return fn


def body(forward, backward, propagator, row_taps, phase_masks, plane_index, wave_ratio, pair_list):
    local_modes, rows, _, width = forward.shape
    waves = wave_ratio.shape[0]
    mode_peers = lax.axis_size("mode")
    row_peers = lax.axis_size("row")
    total = local_modes * mode_peers
    row_total = rows * row_peers
    group_size = total // NG
    half = rows * width

    flat = lambda fields: fields.transpose(0, 2, 1, 3).reshape(fields.shape[0], 2 * half)
    head, last = rounds_of(mode_peers)
    distances = head + last[:2]
    targets, fields = backward, forward
    for distance in head:
        near, far = (targets, fields), [
            swapped(values, "mode", distance) for values in (targets, fields)
        ]
        if targets.ndim > 2:
            near, far = [flat(values) for values in near], [flat(values) for values in far]
        targets, fields = [jnp.concatenate(both, axis=0) for both in zip(near, far)]
    if targets.ndim > 2:
        targets, fields = flat(targets), flat(fields)
    over_even, over_odd = neighbour_rows(targets, width)
    odd = (lax.axis_index("row") % 2).astype(F32)
    taps = jnp.concatenate([row_taps, jnp.full((1, row_taps.shape[1]), odd)], axis=0)
    (both,) = local_call(
        pulled_rows(rows, width),
        [array((targets.shape[0], 4 * half), BF16)],
        [jnp.pad(taps, ((0, 5), (0, 125))), fields, targets, over_even, over_odd],
        flops=24 * targets.shape[0] * half,
    )
    both, pair_list, plane_index, wave_ratio, phase_masks = lax.optimization_barrier(
        (both, pair_list, plane_index, wave_ratio, phase_masks)
    )
    pieces = gathered_last(both, last)

    planes = jnp.arange(phase_masks.shape[0], dtype=jnp.int32)
    selector = (plane_index[:, None] == planes[None, :]).astype(F32)
    picked = jnp.einsum("wp,prc->wrc", selector, phase_masks, precision=lax.Precision.HIGHEST)
    phases = (picked * wave_ratio[:, None, None]).reshape(waves, half)
    cosine = jnp.tile(jnp.cos(phases), (2, 1))
    sine = jnp.tile(jnp.sin(phases), (2, 1))

    places = jnp.arange(total, dtype=jnp.int32)
    peers = lax.axis_index("mode").astype(jnp.int32)
    for k, distance in enumerate(distances):
        peers = peers ^ ((places // (local_modes << k)) % 2 * distance)
    numbers = peers * local_modes + places % local_modes
    groups = numbers // group_size
    to_target = (pair_list[:, 0][:, None] == groups[None, :]).astype(BF16)
    to_forward = (pair_list[:, 1][:, None] == groups[None, :]).astype(BF16)
    mask = lax.dot_general(
        to_forward, to_target, (((0,), (0,)), ((), ())), preferred_element_type=F32
    )
    order = (numbers[:, None] == places[None, :]).astype(BF16)

    early = len(pieces) - 1
    late = len(pieces) - early
    early_total, late_total = early * both.shape[0], late * both.shape[0]
    early_masked, early_spread = local_call(
        masked_and_spread(width),
        [array((2 * early_total, half), BF16)] * 2,
        [cosine, sine, propagator, *pieces[:early]],
        flops=8 * early_total * half * width,
    )
    late_masked, partial = local_call(
        project(width, late),
        [array((2 * late_total, half), BF16), array((total, 2 * total), F32)],
        [cosine, sine, propagator, early_spread, *pieces],
        flops=8 * late_total * half * width + 8 * total * total * half,
    )
    partials = [partial] + [swapped(partial, "row", d) for d in range(row_peers - 1, 0, -1)]
    (back,) = local_call(
        back_propagated(width),
        [array((2 * total, half), BF16)],
        [propagator, *pieces],
        flops=8 * total * half * width,
    )
    arrays = [mask, order, back, early_masked, late_masked, *partials]
    outs = [array((2, local_modes, total), F32), array((waves, rows, width), F32)]
    large = sum(size_of(item) for item in (*arrays, *outs)) > VMEM_BYTES
    first = couple(local_modes, 1.0 / math.sqrt(row_total * width), not large)
    second = gradient(waves, rows, width, -2.0 / total)

    def finish(mask, order, back, early, late, *partials):
        coupling, weights = first(mask, order, *partials)
        return coupling, second(weights, back, early, late)

    coupling, mask_grad = local_call(finish, outs, arrays, flops=8 * total * total * half)
    return coupling, mask_grad


def solution(mesh):
    in_specs = (
        P("mode", "row", None, None),
        P("mode", "row", None, None),
        P(),
        P(),
        P(None, "row", None),
        P(),
        P(),
        P(),
    )
    out_specs = (P(None, "mode", None), P(None, "row", None))
    return jax.shard_map(body, mesh=mesh, in_specs=in_specs, out_specs=out_specs, check_vma=False)
```

```python
import math

import jax
import jax.numpy as jnp
from jax import lax
from jax.experimental import pallas as pl
from jax.experimental.pallas import tpu as pltpu
from jax.sharding import PartitionSpec as P

NG = 16
VMEM_BYTES = 24 << 20
NT = (((1,), (1,)), ((), ()))
F32 = jnp.float32
BF16 = jnp.bfloat16


def size_of(item):
    return math.prod(item.shape) * jnp.dtype(item.dtype).itemsize


def local_call(fn, outs, arrays, flops=0):
    moved = sum(size_of(item) for item in (*arrays, *outs))
    if moved > VMEM_BYTES:
        return fn(*arrays)
    count = len(arrays)

    def kernel(*refs):
        values = fn(*[ref[...] for ref in refs[:count]])
        for ref, value in zip(refs[count:], values):
            ref[...] = value

    return pl.pallas_call(
        kernel,
        out_shape=tuple(outs),
        in_specs=[pl.BlockSpec(memory_space=pltpu.VMEM)] * count,
        out_specs=tuple(pl.BlockSpec(memory_space=pltpu.VMEM) for _ in outs),
        cost_estimate=pl.CostEstimate(flops=flops, bytes_accessed=moved, transcendentals=0),
        compiler_params=pltpu.CompilerParams(vmem_limit_bytes=48 << 20),
    )(*arrays)


def array(shape, dtype):
    return jax.ShapeDtypeStruct(shape, dtype)


def swapped(values, axis, distance):
    peers = lax.axis_size(axis)
    return lax.ppermute(values, axis, [(i, i ^ distance) for i in range(peers)])


def pairs_of(peers, first):
    pairs = [(i, i + 1) for i in range(first, peers - 1, 2)]
    return pairs + [(j, i) for i, j in pairs]


def neighbour_rows(fields, width):
    peers = lax.axis_size("row")
    odd = lax.axis_index("row") % 2 == 1
    half = fields.shape[1] // 2
    row_at = lambda at: jnp.concatenate(
        [fields[:, at : at + width], fields[:, half + at : half + at + width]], axis=1
    )
    first, last = row_at(0), row_at(half - width)
    over_odd = lax.ppermute(jnp.where(odd, last, first), "row", pairs_of(peers, 1))
    over_even = lax.ppermute(jnp.where(odd, first, last), "row", pairs_of(peers, 0))
    return over_even, over_odd


def rounds_of(peers):
    bits = [1 << k for k in reversed(range(peers.bit_length() - 1))]
    head, tail = bits[:-2], bits[-2:]
    last = [tail[0] ^ tail[1], tail[0], tail[1]] if len(tail) == 2 else tail
    return head, last


def gathered_last(values, last):
    return [values] + [swapped(values, "mode", distance) for distance in last]


def pulled_rows(rows, width):
    def fn(taps, fields, own, over_even, over_odd):
        half = rows * width
        odd = jnp.broadcast_to(taps[2:3, 0:1], over_even.shape) > 0.5
        before = jnp.where(odd, over_even.astype(F32), over_odd.astype(F32))
        after = jnp.where(odd, over_odd.astype(F32), over_even.astype(F32))
        real = [before[:, :width]] + [own[:, j * width : (j + 1) * width] for j in range(rows)]
        imag = [before[:, width:]] + [
            own[:, half + j * width : half + (j + 1) * width] for j in range(rows)
        ]
        real = [part.astype(F32) for part in real + [after[:, :width]]]
        imag = [part.astype(F32) for part in imag + [after[:, width:]]]
        out_real, out_imag = [], []
        for j in range(1, rows + 1):
            sources = (j + 1, j, j - 1)
            total_real = total_imag = 0.0
            for k in range(3):
                a, b = taps[0:1, k : k + 1], taps[1:2, k : k + 1]
                total_real = total_real + a * real[sources[k]] + b * imag[sources[k]]
                total_imag = total_imag + a * imag[sources[k]] - b * real[sources[k]]
            out_real.append(total_real)
            out_imag.append(total_imag)
        pulled = jnp.concatenate(out_real + out_imag, axis=1).astype(BF16)
        return (jnp.concatenate([fields, pulled], axis=1),)

    return fn


def parts_of(pieces, first):
    quarter = pieces[0].shape[1] // 4
    cut = lambda at: [piece[:, at * quarter : (at + 1) * quarter] for piece in pieces]
    return jnp.concatenate(cut(first), axis=0), jnp.concatenate(cut(first + 1), axis=0)


def by_rows(values, width):
    return [values[:, at : at + width] for at in range(0, values.shape[1], width)]


def masked_and_spread(width):
    def fn(cosine, sine, propagator, *pieces):
        real, imag = parts_of(pieces, 0)
        total, half = real.shape
        shape = (total // cosine.shape[0], *cosine.shape)
        real = real.astype(F32).reshape(shape)
        imag = imag.astype(F32).reshape(shape)
        masked_real = (real * cosine - imag * sine).reshape(total, half).astype(BF16)
        masked_imag = (real * sine + imag * cosine).reshape(total, half).astype(BF16)
        masked = jnp.concatenate([masked_real, masked_imag], axis=0)
        stacked = jnp.concatenate(by_rows(masked, width), axis=0)
        over_real = jnp.dot(stacked, propagator[0], preferred_element_type=F32)
        over_imag = jnp.dot(stacked, propagator[1], preferred_element_type=F32)
        out_real, out_imag = [], []
        for at in range(0, stacked.shape[0], 2 * total):
            first, second = slice(at, at + total), slice(at + total, at + 2 * total)
            out_real.append(over_real[first] - over_imag[second])
            out_imag.append(over_imag[first] + over_real[second])
        spread = jnp.concatenate(
            [jnp.concatenate(out_real, axis=1), jnp.concatenate(out_imag, axis=1)], axis=0
        )
        return masked, spread.astype(BF16)

    return fn


def both_parts(stacks):
    cut = lambda stack, part: stack[part * (stack.shape[0] // 2) :][: stack.shape[0] // 2]
    return jnp.concatenate([cut(stack, part) for part in (0, 1) for stack in stacks], axis=0)


def project(width, late):
    def fn(cosine, sine, propagator, early_spread, *pieces):
        masked, spread = masked_and_spread(width)(cosine, sine, propagator, *pieces[-late:])
        spread = both_parts([early_spread, spread])
        targets = jnp.concatenate(parts_of(pieces, 2), axis=0)
        total = targets.shape[0] // 2
        product = lax.dot_general(spread, targets, NT, preferred_element_type=F32)
        real = product[:total, :total] + product[total:, total:]
        imag = product[total:, :total] - product[:total, total:]
        return masked, jnp.concatenate([real, imag], axis=1)

    return fn


def back_propagated(width):
    def fn(propagator, *pieces):
        targets = jnp.concatenate(parts_of(pieces, 2), axis=0)
        total = targets.shape[0] // 2
        stacked = jnp.concatenate(by_rows(targets, width), axis=0)
        over_real = lax.dot_general(stacked, propagator[0], NT, preferred_element_type=F32)
        over_imag = lax.dot_general(stacked, propagator[1], NT, preferred_element_type=F32)
        out_real, out_imag = [], []
        for at in range(0, stacked.shape[0], 2 * total):
            first, second = slice(at, at + total), slice(at + total, at + 2 * total)
            out_real.append(over_real[first] + over_imag[second])
            out_imag.append(over_real[second] - over_imag[first])
        result = jnp.concatenate(
            [jnp.concatenate(out_real, axis=1), jnp.concatenate(out_imag, axis=1)], axis=0
        )
        return (result.astype(BF16),)

    return fn


def couple(local_modes, scale_pixels, exact_parts):
    def fn(mask, order, *partials):
        total = mask.shape[0]
        summed = partials[0]
        for part in partials[1:]:
            summed = summed + part
        real = summed[:, :total] * scale_pixels * mask
        imag = summed[:, total:] * scale_pixels * mask
        own = jnp.concatenate([real[:local_modes], imag[:local_modes]], axis=0)
        if exact_parts:
            high = own.astype(BF16)
            rest = own - high.astype(F32)
            middle = rest.astype(BF16)
            low = (rest - middle.astype(F32)).astype(BF16)
            parts = jnp.concatenate([high, middle, low], axis=0)
            parts = jnp.dot(parts, order, preferred_element_type=F32)
            size = own.shape[0]
            own = parts[:size] + parts[size : 2 * size] + parts[2 * size :]
        else:
            own = jnp.dot(own, order.astype(F32), precision=lax.Precision.HIGHEST)
        weight_real, weight_imag = real.astype(BF16), imag.astype(BF16)
        weights = jnp.concatenate(
            [
                jnp.concatenate([weight_real, -weight_imag], axis=1),
                jnp.concatenate([weight_imag, weight_real], axis=1),
            ],
            axis=0,
        )
        return own.reshape(2, local_modes, total), weights

    return fn


def gradient(waves, rows, width, scale_grad):
    def fn(weights, back, early, late):
        total = weights.shape[0] // 2
        adjoint = jnp.dot(weights, back, preferred_element_type=F32)
        fields = both_parts([early, late]).astype(F32)
        term = fields[total:] * adjoint[:total] - fields[:total] * adjoint[total:]
        group = 2 * waves
        folded = jnp.sum(term.reshape(total // group, group, rows * width), axis=0)
        folded = (folded[:waves] + folded[waves:]) * scale_grad
        return jnp.stack(by_rows(folded, width), axis=1)

    return fn


def body(forward, backward, propagator, row_taps, phase_masks, plane_index, wave_ratio, pair_list):
    local_modes, rows, _, width = forward.shape
    waves = wave_ratio.shape[0]
    mode_peers = lax.axis_size("mode")
    row_peers = lax.axis_size("row")
    total = local_modes * mode_peers
    row_total = rows * row_peers
    group_size = total // NG
    half = rows * width

    flat = lambda fields: fields.transpose(0, 2, 1, 3).reshape(fields.shape[0], 2 * half)
    head, last = rounds_of(mode_peers)
    distances = head + last[:2]
    targets, fields = backward, forward
    for distance in head:
        far = [swapped(values, "mode", distance) for values in (targets, fields)]
        if targets.ndim > 2:
            targets, far = flat(targets), [flat(values) for values in far]
            targets = jnp.concatenate([targets, far[0]], axis=0)
            targets, fields = lax.optimization_barrier((targets, fields))
            fields = jnp.concatenate([flat(fields), far[1]], axis=0)
        else:
            targets = jnp.concatenate([targets, far[0]], axis=0)
            fields = jnp.concatenate([fields, far[1]], axis=0)
    if targets.ndim > 2:
        targets, fields = flat(targets), flat(fields)
    over_even, over_odd = neighbour_rows(targets, width)
    odd = (lax.axis_index("row") % 2).astype(F32)
    taps = jnp.concatenate([row_taps, jnp.full((1, row_taps.shape[1]), odd)], axis=0)
    (both,) = local_call(
        pulled_rows(rows, width),
        [array((targets.shape[0], 4 * half), BF16)],
        [jnp.pad(taps, ((0, 5), (0, 125))), fields, targets, over_even, over_odd],
        flops=24 * targets.shape[0] * half,
    )
    both, pair_list, plane_index, wave_ratio, phase_masks = lax.optimization_barrier(
        (both, pair_list, plane_index, wave_ratio, phase_masks)
    )
    pieces = gathered_last(both, last)

    planes = jnp.arange(phase_masks.shape[0], dtype=jnp.int32)
    selector = (plane_index[:, None] == planes[None, :]).astype(F32)
    picked = jnp.einsum("wp,prc->wrc", selector, phase_masks, precision=lax.Precision.HIGHEST)
    phases = (picked * wave_ratio[:, None, None]).reshape(waves, half)
    cosine = jnp.tile(jnp.cos(phases), (2, 1))
    sine = jnp.tile(jnp.sin(phases), (2, 1))

    places = jnp.arange(total, dtype=jnp.int32)
    peers = lax.axis_index("mode").astype(jnp.int32)
    for k, distance in enumerate(distances):
        peers = peers ^ ((places // (local_modes << k)) % 2 * distance)
    numbers = peers * local_modes + places % local_modes
    groups = numbers // group_size
    to_target = (pair_list[:, 0][:, None] == groups[None, :]).astype(BF16)
    to_forward = (pair_list[:, 1][:, None] == groups[None, :]).astype(BF16)
    mask = lax.dot_general(
        to_forward, to_target, (((0,), (0,)), ((), ())), preferred_element_type=F32
    )
    order = (numbers[:, None] == places[None, :]).astype(BF16)

    early = len(pieces) - 1
    late = len(pieces) - early
    early_total, late_total = early * both.shape[0], late * both.shape[0]
    early_masked, early_spread = local_call(
        masked_and_spread(width),
        [array((2 * early_total, half), BF16)] * 2,
        [cosine, sine, propagator, *pieces[:early]],
        flops=8 * early_total * half * width,
    )
    late_masked, partial = local_call(
        project(width, late),
        [array((2 * late_total, half), BF16), array((total, 2 * total), F32)],
        [cosine, sine, propagator, early_spread, *pieces],
        flops=8 * late_total * half * width + 8 * total * total * half,
    )
    partials = [partial] + [swapped(partial, "row", d) for d in range(row_peers - 1, 0, -1)]
    (back,) = local_call(
        back_propagated(width),
        [array((2 * total, half), BF16)],
        [propagator, *pieces],
        flops=8 * total * half * width,
    )
    arrays = [mask, order, back, early_masked, late_masked, *partials]
    outs = [array((2, local_modes, total), F32), array((waves, rows, width), F32)]
    large = sum(size_of(item) for item in (*arrays, *outs)) > VMEM_BYTES
    first = couple(local_modes, 1.0 / math.sqrt(row_total * width), not large)
    second = gradient(waves, rows, width, -2.0 / total)

    def finish(mask, order, back, early, late, *partials):
        coupling, weights = first(mask, order, *partials)
        return coupling, second(weights, back, early, late)

    coupling, mask_grad = local_call(finish, outs, arrays, flops=8 * total * total * half)
    return coupling, mask_grad


def solution(mesh):
    in_specs = (
        P("mode", "row", None, None),
        P("mode", "row", None, None),
        P(),
        P(),
        P(None, "row", None),
        P(),
        P(),
        P(),
    )
    out_specs = (P(None, "mode", None), P(None, "row", None))
    return jax.shard_map(body, mesh=mesh, in_specs=in_specs, out_specs=out_specs, check_vma=False)
```

```python
import math

import jax
import jax.numpy as jnp
from jax import lax
from jax.experimental import pallas as pl
from jax.experimental.pallas import tpu as pltpu
from jax.sharding import PartitionSpec as P

NG = 16
VMEM_BYTES = 24 << 20
NT = (((1,), (1,)), ((), ()))
F32 = jnp.float32
BF16 = jnp.bfloat16


def size_of(item):
    return math.prod(item.shape) * jnp.dtype(item.dtype).itemsize


def local_call(fn, outs, arrays, flops=0):
    moved = sum(size_of(item) for item in (*arrays, *outs))
    if moved > VMEM_BYTES:
        return fn(*arrays)
    count = len(arrays)

    def kernel(*refs):
        values = fn(*[ref[...] for ref in refs[:count]])
        for ref, value in zip(refs[count:], values):
            ref[...] = value

    return pl.pallas_call(
        kernel,
        out_shape=tuple(outs),
        in_specs=[pl.BlockSpec(memory_space=pltpu.VMEM)] * count,
        out_specs=tuple(pl.BlockSpec(memory_space=pltpu.VMEM) for _ in outs),
        cost_estimate=pl.CostEstimate(flops=flops, bytes_accessed=moved, transcendentals=0),
        compiler_params=pltpu.CompilerParams(vmem_limit_bytes=48 << 20),
    )(*arrays)


def array(shape, dtype):
    return jax.ShapeDtypeStruct(shape, dtype)


def swapped(values, axis, distance):
    peers = lax.axis_size(axis)
    return lax.ppermute(values, axis, [(i, i ^ distance) for i in range(peers)])


def pairs_of(peers, first):
    pairs = [(i, i + 1) for i in range(first, peers - 1, 2)]
    return pairs + [(j, i) for i, j in pairs]


def neighbour_rows(fields, width):
    peers = lax.axis_size("row")
    odd = lax.axis_index("row") % 2 == 1
    half = fields.shape[1] // 2
    row_at = lambda at: jnp.concatenate(
        [fields[:, at : at + width], fields[:, half + at : half + at + width]], axis=1
    )
    first, last = row_at(0), row_at(half - width)
    over_odd = lax.ppermute(jnp.where(odd, last, first), "row", pairs_of(peers, 1))
    over_even = lax.ppermute(jnp.where(odd, first, last), "row", pairs_of(peers, 0))
    return over_even, over_odd


def rounds_of(peers):
    bits = [1 << k for k in reversed(range(peers.bit_length() - 1))]
    head, tail = bits[:-2], bits[-2:]
    last = [tail[1], tail[0] ^ tail[1], tail[0]] if len(tail) == 2 else tail
    return head, last


def gathered_last(values, last):
    return [values] + [swapped(values, "mode", distance) for distance in last]


def pulled_rows(rows, width):
    def fn(taps, fields, own, over_even, over_odd):
        half = rows * width
        odd = jnp.broadcast_to(taps[2:3, 0:1], over_even.shape) > 0.5
        before = jnp.where(odd, over_even.astype(F32), over_odd.astype(F32))
        after = jnp.where(odd, over_odd.astype(F32), over_even.astype(F32))
        real = [before[:, :width]] + [own[:, j * width : (j + 1) * width] for j in range(rows)]
        imag = [before[:, width:]] + [
            own[:, half + j * width : half + (j + 1) * width] for j in range(rows)
        ]
        real = [part.astype(F32) for part in real + [after[:, :width]]]
        imag = [part.astype(F32) for part in imag + [after[:, width:]]]
        out_real, out_imag = [], []
        for j in range(1, rows + 1):
            sources = (j + 1, j, j - 1)
            total_real = total_imag = 0.0
            for k in range(3):
                a, b = taps[0:1, k : k + 1], taps[1:2, k : k + 1]
                total_real = total_real + a * real[sources[k]] + b * imag[sources[k]]
                total_imag = total_imag + a * imag[sources[k]] - b * real[sources[k]]
            out_real.append(total_real)
            out_imag.append(total_imag)
        pulled = jnp.concatenate(out_real + out_imag, axis=1).astype(BF16)
        return (jnp.concatenate([fields, pulled], axis=1),)

    return fn


def parts_of(pieces, first):
    quarter = pieces[0].shape[1] // 4
    cut = lambda at: [piece[:, at * quarter : (at + 1) * quarter] for piece in pieces]
    return jnp.concatenate(cut(first), axis=0), jnp.concatenate(cut(first + 1), axis=0)


def by_rows(values, width):
    return [values[:, at : at + width] for at in range(0, values.shape[1], width)]


def masked_and_spread(width):
    def fn(cosine, sine, propagator, *pieces):
        real, imag = parts_of(pieces, 0)
        total, half = real.shape
        shape = (total // cosine.shape[0], *cosine.shape)
        real = real.astype(F32).reshape(shape)
        imag = imag.astype(F32).reshape(shape)
        masked_real = (real * cosine - imag * sine).reshape(total, half).astype(BF16)
        masked_imag = (real * sine + imag * cosine).reshape(total, half).astype(BF16)
        masked = jnp.concatenate([masked_real, masked_imag], axis=0)
        stacked = jnp.concatenate(by_rows(masked, width), axis=0)
        over_real = jnp.dot(stacked, propagator[0], preferred_element_type=F32)
        over_imag = jnp.dot(stacked, propagator[1], preferred_element_type=F32)
        out_real, out_imag = [], []
        for at in range(0, stacked.shape[0], 2 * total):
            first, second = slice(at, at + total), slice(at + total, at + 2 * total)
            out_real.append(over_real[first] - over_imag[second])
            out_imag.append(over_imag[first] + over_real[second])
        spread = jnp.concatenate(
            [jnp.concatenate(out_real, axis=1), jnp.concatenate(out_imag, axis=1)], axis=0
        )
        return masked, spread.astype(BF16)

    return fn


def both_parts(stacks):
    cut = lambda stack, part: stack[part * (stack.shape[0] // 2) :][: stack.shape[0] // 2]
    return jnp.concatenate([cut(stack, part) for part in (0, 1) for stack in stacks], axis=0)


def project(width, late):
    def fn(cosine, sine, propagator, early_spread, *pieces):
        masked, spread = masked_and_spread(width)(cosine, sine, propagator, *pieces[-late:])
        spread = both_parts([early_spread, spread])
        targets = jnp.concatenate(parts_of(pieces, 2), axis=0)
        total = targets.shape[0] // 2
        product = lax.dot_general(spread, targets, NT, preferred_element_type=F32)
        real = product[:total, :total] + product[total:, total:]
        imag = product[total:, :total] - product[:total, total:]
        return masked, jnp.concatenate([real, imag], axis=1)

    return fn


def back_propagated(width):
    def fn(propagator, *pieces):
        targets = jnp.concatenate(parts_of(pieces, 2), axis=0)
        total = targets.shape[0] // 2
        stacked = jnp.concatenate(by_rows(targets, width), axis=0)
        over_real = lax.dot_general(stacked, propagator[0], NT, preferred_element_type=F32)
        over_imag = lax.dot_general(stacked, propagator[1], NT, preferred_element_type=F32)
        out_real, out_imag = [], []
        for at in range(0, stacked.shape[0], 2 * total):
            first, second = slice(at, at + total), slice(at + total, at + 2 * total)
            out_real.append(over_real[first] + over_imag[second])
            out_imag.append(over_real[second] - over_imag[first])
        result = jnp.concatenate(
            [jnp.concatenate(out_real, axis=1), jnp.concatenate(out_imag, axis=1)], axis=0
        )
        return (result.astype(BF16),)

    return fn


def couple(local_modes, scale_pixels, exact_parts):
    def fn(mask, order, *partials):
        total = mask.shape[0]
        summed = partials[0]
        for part in partials[1:]:
            summed = summed + part
        real = summed[:, :total] * scale_pixels * mask
        imag = summed[:, total:] * scale_pixels * mask
        own = jnp.concatenate([real[:local_modes], imag[:local_modes]], axis=0)
        if exact_parts:
            high = own.astype(BF16)
            rest = own - high.astype(F32)
            middle = rest.astype(BF16)
            low = (rest - middle.astype(F32)).astype(BF16)
            parts = jnp.concatenate([high, middle, low], axis=0)
            parts = jnp.dot(parts, order, preferred_element_type=F32)
            size = own.shape[0]
            own = parts[:size] + parts[size : 2 * size] + parts[2 * size :]
        else:
            own = jnp.dot(own, order.astype(F32), precision=lax.Precision.HIGHEST)
        weight_real, weight_imag = real.astype(BF16), imag.astype(BF16)
        weights = jnp.concatenate(
            [
                jnp.concatenate([weight_real, -weight_imag], axis=1),
                jnp.concatenate([weight_imag, weight_real], axis=1),
            ],
            axis=0,
        )
        return own.reshape(2, local_modes, total), weights

    return fn


def gradient(waves, rows, width, scale_grad):
    def fn(weights, back, early, late):
        total = weights.shape[0] // 2
        adjoint = jnp.dot(weights, back, preferred_element_type=F32)
        fields = both_parts([early, late]).astype(F32)
        term = fields[total:] * adjoint[:total] - fields[:total] * adjoint[total:]
        group = 2 * waves
        folded = jnp.sum(term.reshape(total // group, group, rows * width), axis=0)
        folded = (folded[:waves] + folded[waves:]) * scale_grad
        return jnp.stack(by_rows(folded, width), axis=1)

    return fn


def body(forward, backward, propagator, row_taps, phase_masks, plane_index, wave_ratio, pair_list):
    local_modes, rows, _, width = forward.shape
    waves = wave_ratio.shape[0]
    mode_peers = lax.axis_size("mode")
    row_peers = lax.axis_size("row")
    total = local_modes * mode_peers
    row_total = rows * row_peers
    group_size = total // NG
    half = rows * width

    flat = lambda fields: fields.transpose(0, 2, 1, 3).reshape(fields.shape[0], 2 * half)
    head, last = rounds_of(mode_peers)
    distances = head + last[:2]
    targets, fields = backward, forward
    for distance in head:
        near, far = (targets, fields), [
            swapped(values, "mode", distance) for values in (targets, fields)
        ]
        if targets.ndim > 2:
            near, far = [flat(values) for values in near], [flat(values) for values in far]
        targets, fields = [jnp.concatenate(both, axis=0) for both in zip(near, far)]
    if targets.ndim > 2:
        targets, fields = flat(targets), flat(fields)
    over_even, over_odd = neighbour_rows(targets, width)
    odd = (lax.axis_index("row") % 2).astype(F32)
    taps = jnp.concatenate([row_taps, jnp.full((1, row_taps.shape[1]), odd)], axis=0)
    (both,) = local_call(
        pulled_rows(rows, width),
        [array((targets.shape[0], 4 * half), BF16)],
        [jnp.pad(taps, ((0, 5), (0, 125))), fields, targets, over_even, over_odd],
        flops=24 * targets.shape[0] * half,
    )
    both, pair_list, plane_index, wave_ratio, phase_masks = lax.optimization_barrier(
        (both, pair_list, plane_index, wave_ratio, phase_masks)
    )
    pieces = gathered_last(both, last)

    planes = jnp.arange(phase_masks.shape[0], dtype=jnp.int32)
    selector = (plane_index[:, None] == planes[None, :]).astype(F32)
    picked = jnp.einsum("wp,prc->wrc", selector, phase_masks, precision=lax.Precision.HIGHEST)
    phases = (picked * wave_ratio[:, None, None]).reshape(waves, half)
    cosine = jnp.tile(jnp.cos(phases), (2, 1))
    sine = jnp.tile(jnp.sin(phases), (2, 1))

    places = jnp.arange(total, dtype=jnp.int32)
    peers = lax.axis_index("mode").astype(jnp.int32)
    for k, distance in enumerate(distances):
        peers = peers ^ ((places // (local_modes << k)) % 2 * distance)
    numbers = peers * local_modes + places % local_modes
    groups = numbers // group_size
    to_target = (pair_list[:, 0][:, None] == groups[None, :]).astype(BF16)
    to_forward = (pair_list[:, 1][:, None] == groups[None, :]).astype(BF16)
    mask = lax.dot_general(
        to_forward, to_target, (((0,), (0,)), ((), ())), preferred_element_type=F32
    )
    order = (numbers[:, None] == places[None, :]).astype(BF16)

    early = (len(pieces) + 1) // 2
    late = len(pieces) - early
    early_total, late_total = early * both.shape[0], late * both.shape[0]
    early_masked, early_spread = local_call(
        masked_and_spread(width),
        [array((2 * early_total, half), BF16)] * 2,
        [cosine, sine, propagator, *pieces[:early]],
        flops=8 * early_total * half * width,
    )
    late_masked, partial = local_call(
        project(width, late),
        [array((2 * late_total, half), BF16), array((total, 2 * total), F32)],
        [cosine, sine, propagator, early_spread, *pieces],
        flops=8 * late_total * half * width + 8 * total * total * half,
    )
    partials = [partial] + [swapped(partial, "row", d) for d in range(row_peers - 1, 0, -1)]
    (back,) = local_call(
        back_propagated(width),
        [array((2 * total, half), BF16)],
        [propagator, *pieces],
        flops=8 * total * half * width,
    )
    arrays = [mask, order, back, early_masked, late_masked, *partials]
    outs = [array((2, local_modes, total), F32), array((waves, rows, width), F32)]
    large = sum(size_of(item) for item in (*arrays, *outs)) > VMEM_BYTES
    first = couple(local_modes, 1.0 / math.sqrt(row_total * width), not large)
    second = gradient(waves, rows, width, -2.0 / total)

    def finish(mask, order, back, early, late, *partials):
        coupling, weights = first(mask, order, *partials)
        return coupling, second(weights, back, early, late)

    coupling, mask_grad = local_call(finish, outs, arrays, flops=8 * total * total * half)
    return coupling, mask_grad


def solution(mesh):
    in_specs = (
        P("mode", "row", None, None),
        P("mode", "row", None, None),
        P(),
        P(),
        P(None, "row", None),
        P(),
        P(),
        P(),
    )
    out_specs = (P(None, "mode", None), P(None, "row", None))
    return jax.shard_map(body, mesh=mesh, in_specs=in_specs, out_specs=out_specs, check_vma=False)
```

```python
import math

import jax
import jax.numpy as jnp
from jax import lax
from jax.experimental import pallas as pl
from jax.experimental.pallas import tpu as pltpu
from jax.sharding import PartitionSpec as P

NG = 16
VMEM_BYTES = 24 << 20
NT = (((1,), (1,)), ((), ()))
F32 = jnp.float32
BF16 = jnp.bfloat16


def size_of(item):
    return math.prod(item.shape) * jnp.dtype(item.dtype).itemsize


def local_call(fn, outs, arrays, flops=0):
    moved = sum(size_of(item) for item in (*arrays, *outs))
    if moved > VMEM_BYTES:
        return fn(*arrays)
    count = len(arrays)

    def kernel(*refs):
        values = fn(*[ref[...] for ref in refs[:count]])
        for ref, value in zip(refs[count:], values):
            ref[...] = value

    return pl.pallas_call(
        kernel,
        out_shape=tuple(outs),
        in_specs=[pl.BlockSpec(memory_space=pltpu.VMEM)] * count,
        out_specs=tuple(pl.BlockSpec(memory_space=pltpu.VMEM) for _ in outs),
        cost_estimate=pl.CostEstimate(flops=flops, bytes_accessed=moved, transcendentals=0),
        compiler_params=pltpu.CompilerParams(vmem_limit_bytes=48 << 20),
    )(*arrays)


def array(shape, dtype):
    return jax.ShapeDtypeStruct(shape, dtype)


def swapped(values, axis, distance):
    peers = lax.axis_size(axis)
    return lax.ppermute(values, axis, [(i, i ^ distance) for i in range(peers)])


def pairs_of(peers, first):
    pairs = [(i, i + 1) for i in range(first, peers - 1, 2)]
    return pairs + [(j, i) for i, j in pairs]


def neighbour_rows(fields, width):
    peers = lax.axis_size("row")
    odd = lax.axis_index("row") % 2 == 1
    half = fields.shape[1] // 2
    row_at = lambda at: jnp.concatenate(
        [fields[:, at : at + width], fields[:, half + at : half + at + width]], axis=1
    )
    first, last = row_at(0), row_at(half - width)
    over_odd = lax.ppermute(jnp.where(odd, last, first), "row", pairs_of(peers, 1))
    over_even = lax.ppermute(jnp.where(odd, first, last), "row", pairs_of(peers, 0))
    return over_even, over_odd


def rounds_of(peers):
    bits = [1 << k for k in reversed(range(peers.bit_length() - 1))]
    head, tail = bits[:-2], bits[-2:]
    last = [tail[0] ^ tail[1], tail[1], tail[0]] if len(tail) == 2 else tail
    return head, last


def gathered_last(values, last):
    return [values] + [swapped(values, "mode", distance) for distance in last]


def pulled_rows(rows, width):
    def fn(taps, fields, own, over_even, over_odd):
        half = rows * width
        odd = jnp.broadcast_to(taps[2:3, 0:1], over_even.shape) > 0.5
        before = jnp.where(odd, over_even.astype(F32), over_odd.astype(F32))
        after = jnp.where(odd, over_odd.astype(F32), over_even.astype(F32))
        real = [before[:, :width]] + [own[:, j * width : (j + 1) * width] for j in range(rows)]
        imag = [before[:, width:]] + [
            own[:, half + j * width : half + (j + 1) * width] for j in range(rows)
        ]
        real = [part.astype(F32) for part in real + [after[:, :width]]]
        imag = [part.astype(F32) for part in imag + [after[:, width:]]]
        out_real, out_imag = [], []
        for j in range(1, rows + 1):
            sources = (j + 1, j, j - 1)
            total_real = total_imag = 0.0
            for k in range(3):
                a, b = taps[0:1, k : k + 1], taps[1:2, k : k + 1]
                total_real = total_real + a * real[sources[k]] + b * imag[sources[k]]
                total_imag = total_imag + a * imag[sources[k]] - b * real[sources[k]]
            out_real.append(total_real)
            out_imag.append(total_imag)
        pulled = jnp.concatenate(out_real + out_imag, axis=1).astype(BF16)
        return (jnp.concatenate([fields, pulled], axis=1),)

    return fn


def parts_of(pieces, first):
    quarter = pieces[0].shape[1] // 4
    cut = lambda at: [piece[:, at * quarter : (at + 1) * quarter] for piece in pieces]
    return jnp.concatenate(cut(first), axis=0), jnp.concatenate(cut(first + 1), axis=0)


def by_rows(values, width):
    return [values[:, at : at + width] for at in range(0, values.shape[1], width)]


def masked_and_spread(width):
    def fn(cosine, sine, propagator, *pieces):
        real, imag = parts_of(pieces, 0)
        total, half = real.shape
        shape = (total // cosine.shape[0], *cosine.shape)
        real = real.astype(F32).reshape(shape)
        imag = imag.astype(F32).reshape(shape)
        masked_real = (real * cosine - imag * sine).reshape(total, half).astype(BF16)
        masked_imag = (real * sine + imag * cosine).reshape(total, half).astype(BF16)
        masked = jnp.concatenate([masked_real, masked_imag], axis=0)
        stacked = jnp.concatenate(by_rows(masked, width), axis=0)
        over_real = jnp.dot(stacked, propagator[0], preferred_element_type=F32)
        over_imag = jnp.dot(stacked, propagator[1], preferred_element_type=F32)
        out_real, out_imag = [], []
        for at in range(0, stacked.shape[0], 2 * total):
            first, second = slice(at, at + total), slice(at + total, at + 2 * total)
            out_real.append(over_real[first] - over_imag[second])
            out_imag.append(over_imag[first] + over_real[second])
        spread = jnp.concatenate(
            [jnp.concatenate(out_real, axis=1), jnp.concatenate(out_imag, axis=1)], axis=0
        )
        return masked, spread.astype(BF16)

    return fn


def both_parts(stacks):
    cut = lambda stack, part: stack[part * (stack.shape[0] // 2) :][: stack.shape[0] // 2]
    return jnp.concatenate([cut(stack, part) for part in (0, 1) for stack in stacks], axis=0)


def project(width, late):
    def fn(cosine, sine, propagator, early_spread, *pieces):
        masked, spread = masked_and_spread(width)(cosine, sine, propagator, *pieces[-late:])
        spread = both_parts([early_spread, spread])
        targets = jnp.concatenate(parts_of(pieces, 2), axis=0)
        total = targets.shape[0] // 2
        product = lax.dot_general(spread, targets, NT, preferred_element_type=F32)
        real = product[:total, :total] + product[total:, total:]
        imag = product[total:, :total] - product[:total, total:]
        return masked, jnp.concatenate([real, imag], axis=1)

    return fn


def back_propagated(width):
    def fn(propagator, *pieces):
        targets = jnp.concatenate(parts_of(pieces, 2), axis=0)
        total = targets.shape[0] // 2
        stacked = jnp.concatenate(by_rows(targets, width), axis=0)
        over_real = lax.dot_general(stacked, propagator[0], NT, preferred_element_type=F32)
        over_imag = lax.dot_general(stacked, propagator[1], NT, preferred_element_type=F32)
        out_real, out_imag = [], []
        for at in range(0, stacked.shape[0], 2 * total):
            first, second = slice(at, at + total), slice(at + total, at + 2 * total)
            out_real.append(over_real[first] + over_imag[second])
            out_imag.append(over_real[second] - over_imag[first])
        result = jnp.concatenate(
            [jnp.concatenate(out_real, axis=1), jnp.concatenate(out_imag, axis=1)], axis=0
        )
        return (result.astype(BF16),)

    return fn


def couple(local_modes, scale_pixels, exact_parts):
    def fn(mask, order, *partials):
        total = mask.shape[0]
        summed = partials[0]
        for part in partials[1:]:
            summed = summed + part
        real = summed[:, :total] * scale_pixels * mask
        imag = summed[:, total:] * scale_pixels * mask
        own = jnp.concatenate([real[:local_modes], imag[:local_modes]], axis=0)
        if exact_parts:
            high = own.astype(BF16)
            rest = own - high.astype(F32)
            middle = rest.astype(BF16)
            low = (rest - middle.astype(F32)).astype(BF16)
            parts = jnp.concatenate([high, middle, low], axis=0)
            parts = jnp.dot(parts, order, preferred_element_type=F32)
            size = own.shape[0]
            own = parts[:size] + parts[size : 2 * size] + parts[2 * size :]
        else:
            own = jnp.dot(own, order.astype(F32), precision=lax.Precision.HIGHEST)
        weight_real, weight_imag = real.astype(BF16), imag.astype(BF16)
        weights = jnp.concatenate(
            [
                jnp.concatenate([weight_real, -weight_imag], axis=1),
                jnp.concatenate([weight_imag, weight_real], axis=1),
            ],
            axis=0,
        )
        return own.reshape(2, local_modes, total), weights

    return fn


def gradient(waves, rows, width, scale_grad):
    def fn(weights, back, early, late):
        total = weights.shape[0] // 2
        adjoint = jnp.dot(weights, back, preferred_element_type=F32)
        fields = both_parts([early, late]).astype(F32)
        term = fields[total:] * adjoint[:total] - fields[:total] * adjoint[total:]
        group = 2 * waves
        folded = jnp.sum(term.reshape(total // group, group, rows * width), axis=0)
        folded = (folded[:waves] + folded[waves:]) * scale_grad
        return jnp.stack(by_rows(folded, width), axis=1)

    return fn


def body(forward, backward, propagator, row_taps, phase_masks, plane_index, wave_ratio, pair_list):
    local_modes, rows, _, width = forward.shape
    waves = wave_ratio.shape[0]
    mode_peers = lax.axis_size("mode")
    row_peers = lax.axis_size("row")
    total = local_modes * mode_peers
    row_total = rows * row_peers
    group_size = total // NG
    half = rows * width

    flat = lambda fields: fields.transpose(0, 2, 1, 3).reshape(fields.shape[0], 2 * half)
    head, last = rounds_of(mode_peers)
    distances = head + last[:2]
    targets, fields = backward, forward
    for distance in head:
        near, far = (targets, fields), [
            swapped(values, "mode", distance) for values in (targets, fields)
        ]
        if targets.ndim > 2:
            near, far = [flat(values) for values in near], [flat(values) for values in far]
        targets, fields = [jnp.concatenate(both, axis=0) for both in zip(near, far)]
    if targets.ndim > 2:
        targets, fields = flat(targets), flat(fields)
    over_even, over_odd = neighbour_rows(targets, width)
    odd = (lax.axis_index("row") % 2).astype(F32)
    taps = jnp.concatenate([row_taps, jnp.full((1, row_taps.shape[1]), odd)], axis=0)
    (both,) = local_call(
        pulled_rows(rows, width),
        [array((targets.shape[0], 4 * half), BF16)],
        [jnp.pad(taps, ((0, 5), (0, 125))), fields, targets, over_even, over_odd],
        flops=24 * targets.shape[0] * half,
    )
    both, pair_list, plane_index, wave_ratio, phase_masks = lax.optimization_barrier(
        (both, pair_list, plane_index, wave_ratio, phase_masks)
    )
    pieces = gathered_last(both, last)

    planes = jnp.arange(phase_masks.shape[0], dtype=jnp.int32)
    selector = (plane_index[:, None] == planes[None, :]).astype(F32)
    picked = jnp.einsum("wp,prc->wrc", selector, phase_masks, precision=lax.Precision.HIGHEST)
    phases = (picked * wave_ratio[:, None, None]).reshape(waves, half)
    cosine = jnp.tile(jnp.cos(phases), (2, 1))
    sine = jnp.tile(jnp.sin(phases), (2, 1))

    places = jnp.arange(total, dtype=jnp.int32)
    peers = lax.axis_index("mode").astype(jnp.int32)
    for k, distance in enumerate(distances):
        peers = peers ^ ((places // (local_modes << k)) % 2 * distance)
    numbers = peers * local_modes + places % local_modes
    groups = numbers // group_size
    to_target = (pair_list[:, 0][:, None] == groups[None, :]).astype(BF16)
    to_forward = (pair_list[:, 1][:, None] == groups[None, :]).astype(BF16)
    mask = lax.dot_general(
        to_forward, to_target, (((0,), (0,)), ((), ())), preferred_element_type=F32
    )
    order = (numbers[:, None] == places[None, :]).astype(BF16)

    early = len(pieces) - 1
    late = len(pieces) - early
    early_total, late_total = early * both.shape[0], late * both.shape[0]
    early_masked, early_spread = local_call(
        masked_and_spread(width),
        [array((2 * early_total, half), BF16)] * 2,
        [cosine, sine, propagator, *pieces[:early]],
        flops=8 * early_total * half * width,
    )
    late_masked, partial = local_call(
        project(width, late),
        [array((2 * late_total, half), BF16), array((total, 2 * total), F32)],
        [cosine, sine, propagator, early_spread, *pieces],
        flops=8 * late_total * half * width + 8 * total * total * half,
    )
    partials = [partial] + [swapped(partial, "row", d) for d in range(row_peers - 1, 0, -1)]
    (back,) = local_call(
        back_propagated(width),
        [array((2 * total, half), BF16)],
        [propagator, *pieces],
        flops=8 * total * half * width,
    )
    arrays = [mask, order, back, early_masked, late_masked, *partials]
    outs = [array((2, local_modes, total), F32), array((waves, rows, width), F32)]
    large = sum(size_of(item) for item in (*arrays, *outs)) > VMEM_BYTES
    first = couple(local_modes, 1.0 / math.sqrt(row_total * width), not large)
    second = gradient(waves, rows, width, -2.0 / total)

    def finish(mask, order, back, early, late, *partials):
        coupling, weights = first(mask, order, *partials)
        return coupling, second(weights, back, early, late)

    coupling, mask_grad = local_call(finish, outs, arrays, flops=8 * total * total * half)
    return coupling, mask_grad


def solution(mesh):
    in_specs = (
        P("mode", "row", None, None),
        P("mode", "row", None, None),
        P(),
        P(),
        P(None, "row", None),
        P(),
        P(),
        P(),
    )
    out_specs = (P(None, "mode", None), P(None, "row", None))
    return jax.shard_map(body, mesh=mesh, in_specs=in_specs, out_specs=out_specs, check_vma=False)
```
